32 devices in a mesh: group: 2 (over x), seq: 8 (over z, y), clip: 2 (over core).
Axes of the slice: x: 2, y: 2, z: 4, core: 2. Of those that a mesh axis runs over, the one named last changes fastest.
Arguments:
- latent: float32 [4, 8, 256, 128], P(('group', 'clip'), 'seq'), parts along dimension 0, may hold values from -6 to 6
- context: float32 [4, 8, 256, 128], P(('group', 'clip'), 'seq'), parts along dimension 0, may hold values from -6 to 6
- frozen: int32 [16], P('group'), parts along dimension 0, may hold values 0 or 1
- read_list: int32 [16, 3], P('group'), parts along dimension 0, may hold values from -1 to 6, as said below
- w_embed: bfloat16 [128, 1536], replicated, may hold values from -0.5 to 0.5
- w_qkv: bfloat16 [3, 1536, 1536], P(None, None, 'clip')
- w_attn_out: bfloat16 [1536, 1536], P('clip'), may hold values from -0.45898438 to 0.45898438
- w_head: bfloat16 [1536, 256], replicated, may hold values from -0.15625 to 0.15625
Outputs:
- mirrored: float32 [4, 8, 256, 128], P(('group', 'clip'), 'seq'), parts along dimension 0
The draws below stay inside these ranges and needn't reach their ends.
There are 2 independent parts, one for each index of `group`. The reference program is written for one: setup_inputs(seed, part) draws one part's arguments, and reference() takes and returns one part's arrays. A program takes and returns all parts, laid end to end along the dimension named above; an argument that names none is the same for every part. Nothing has to cross between parts.
Inputs may be any that keep to these rules, and one draw needn't show every extreme that they name: `read_list`: row f lists min(f, 3) distinct earlier frames, the first of them f - 1, and -1 in the remaining entries.
All inputs are finite; a program needn't handle non-finite values.
Results may differ from the reference program's by a relative error of at most 0.015.
Values may be sent and summed in bfloat16 or wider, within the bound.
No kernel may reach another device: no remote copies, remote signals or barrier semaphores. Data moves between devices by JAX's collectives and lax.ppermute only.
A program may use at most 128 MiB of HBM per device.

```python
import math
import jax
import jax.numpy as jnp
from jax import lax

D = 1536
HD = 128
C = 128
TOK = 256
LINKS = 3
SWEEPS = 2
FRAMES = 8
CLIPS = 2


def draw_read_list(key, part):
    frame_ids = jnp.arange(FRAMES, dtype=jnp.int32)[:, None]
    earlier = jnp.arange(FRAMES, dtype=jnp.int32)[None, :]
    noise = jax.random.randint(jax.random.fold_in(key, 11), (FRAMES, FRAMES), 0, 2 ** 20, dtype=jnp.int32) * FRAMES + earlier
    usable = earlier < frame_ids - 1
    scores = jnp.where(usable, noise, -1 - earlier)
    top_values, picks = lax.top_k(scores, LINKS - 1)
    picks = jnp.where(top_values >= 0, picks.astype(jnp.int32), -1)
    first = jnp.where(frame_ids >= 1, frame_ids - 1, -1)
    return jnp.concatenate([first, picks], axis=1).astype(jnp.int32)


def draw_w_qkv(key, part):
    base = jax.random.normal(jax.random.fold_in(key, 21), (3, D, D), jnp.float32) * D ** (-0.5)
    gains = jnp.exp(jax.random.uniform(jax.random.fold_in(key, 22), (D // HD,), jnp.float32, 0.0, math.log(4.0)))
    queries = base[0] * jnp.repeat(gains, HD)[None, :]
    return jnp.concatenate([queries[None], base[1:]], axis=0).astype(jnp.bfloat16)


def with_ends(entries, rng, least, top_value):
    place = [jax.random.randint(jax.random.fold_in(rng, axis), (), 0, length) for axis, length in enumerate(entries.shape)]
    main_axis = entries.shape.index(max(entries.shape))
    next_to = place[:main_axis] + [(place[main_axis] + 1) % entries.shape[main_axis]] + place[main_axis + 1:]
    return entries.at[tuple(place)].set(least).at[tuple(next_to)].set(top_value)


def level_of(rng, dims, cuts, least, largest):
    level, own = 1.0, jax.random.fold_in(rng, 6)
    for position, parts in cuts:
        steps = jnp.exp(jax.random.uniform(jax.random.fold_in(own, position), (parts,), jnp.float32, least / len(cuts), largest / len(cuts)))
        level = level * jnp.repeat(steps, dims[position] // parts).reshape([-1 if axis == position else 1 for axis in range(len(dims))])
    return level


def scatter_about(stream_key, extent, spread, limit, cuts=(), kind=jnp.bfloat16):
    values = spread * jax.random.normal(stream_key, extent, jnp.float32)
    if cuts:
        values = values * level_of(stream_key, extent, cuts, -0.22, 0.18)
    return jnp.clip(values, -limit, limit).astype(kind)


def setup_inputs(seed: int = 0, part: int = 0) -> dict:
    keys = jax.random.split(jax.random.key(seed), 9)
    part_splits = jax.random.split(jax.random.fold_in(keys[8], part), 9)
    return {
        "latent": scatter_about(part_splits[0], (CLIPS, FRAMES, TOK, C), 1.0, 6.0, ((0, 2), (1, 8)), jnp.float32),
        "context": scatter_about(part_splits[1], (CLIPS, FRAMES, TOK, C), 1.0, 6.0, ((0, 2), (1, 8)), jnp.float32),
        "frozen": with_ends((jax.random.randint(part_splits[2], (FRAMES,), 0, 3) < 1).astype(jnp.int32), jax.random.fold_in(part_splits[2], 1), 0, 1),
        "read_list": draw_read_list(jax.random.fold_in(jax.random.fold_in(keys[8], part), 71), part),
        "w_embed": scatter_about(keys[4], (C, D), C ** -0.5, 0.5),
        "w_qkv": draw_w_qkv(jax.random.fold_in(keys[8], 71), part),
        "w_attn_out": scatter_about(keys[6], (D, D), (3.0 * D ** -0.5), 0.45898438, ((0, 2),)),
        "w_head": scatter_about(keys[7], (D, 2 * C), D ** -0.5, 0.15625),
    }


EPSILON = 1e-05
MASKED_SCORE = -1e+30

def normalize(values):
    average = lax.optimization_barrier(jnp.mean(values, axis=-1, keepdims=True))
    centred = values - average
    spread_sq = lax.optimization_barrier(jnp.mean(centred * centred, axis=-1, keepdims=True))
    return centred * lax.rsqrt(spread_sq + EPSILON)

def widen(values):
    return lax.optimization_barrier(values.astype(jnp.bfloat16)).astype(jnp.float32)

def predict(current, read_list, w_embed, w_qkv, w_attn_out, w_head):
    exact_mode = lax.Precision.HIGHEST
    embedded = jnp.einsum('cftk,kd->cftd', widen(current), w_embed.astype(jnp.float32), precision=exact_mode)
    normed = widen(normalize(embedded))
    projected = jnp.einsum('cftd,jde->jcfte', normed, w_qkv.astype(jnp.float32), precision=exact_mode).astype(jnp.bfloat16)
    queries = projected[0]
    key_rows = projected[1]
    value_rows = projected[2]
    clip_count, frames, tokens, model_width = queries.shape
    head_count = model_width // HD

    def one_frame(frame_index):
        picked = read_list[frame_index]
        usable = picked >= 0
        clamped = jnp.maximum(picked, 0).astype(jnp.int32)
        own_keys = lax.dynamic_index_in_dim(key_rows, frame_index, 1, keepdims=True)
        own_values = lax.dynamic_index_in_dim(value_rows, frame_index, 1, keepdims=True)
        far_keys = jnp.take(key_rows, clamped, axis=1)
        far_values = jnp.take(value_rows, clamped, axis=1)
        key_all = jnp.concatenate([own_keys, far_keys], axis=1).reshape(clip_count, -1, head_count, HD).astype(jnp.float32)
        value_all = jnp.concatenate([own_values, far_values], axis=1).reshape(clip_count, -1, head_count, HD).astype(jnp.float32)
        query_rows = lax.dynamic_index_in_dim(queries, frame_index, 1, keepdims=False)
        query_rows = query_rows.reshape(clip_count, tokens, head_count, HD).astype(jnp.float32)
        scores = jnp.einsum('cqhd,ckhd->chqk', query_rows, key_all, precision=exact_mode) * (1.0 / math.sqrt(HD))
        allowed = jnp.repeat(jnp.concatenate([jnp.ones((1,), dtype=jnp.bool_), usable]), tokens)
        scores = jnp.where(allowed, scores, MASKED_SCORE)
        weights = widen(jax.nn.softmax(scores, axis=-1))
        attended = jnp.einsum('chqk,ckhd->cqhd', weights, value_all, precision=exact_mode)
        return attended.astype(jnp.bfloat16).reshape(clip_count, tokens, model_width)
    attended = lax.map(one_frame, jnp.arange(frames, dtype=jnp.int32))
    attended = jnp.transpose(attended, (1, 0, 2, 3)).astype(jnp.float32)
    residual = embedded + jnp.einsum('cftd,de->cfte', attended, w_attn_out.astype(jnp.float32), precision=exact_mode)
    head_in = widen(normalize(residual))
    return jnp.einsum('cftd,de->cfte', head_in, w_head.astype(jnp.float32), precision=exact_mode)

def reference(latent, context, frozen, read_list, w_embed, w_qkv, w_attn_out, w_head):
    frozen_mask = (frozen == 1)[None, :, None, None]
    current = jnp.where(frozen_mask, context, latent)
    for sweep_index in range(SWEEPS):
        predicted = predict(current, read_list, w_embed, w_qkv, w_attn_out, w_head)
        previous = jnp.concatenate([jnp.zeros_like(predicted[:, :1]), predicted[:, :-1]], axis=1)
        moved = latent * jnp.exp(jnp.tanh(previous[..., C:])) + previous[..., :C]
        current = jnp.where(frozen_mask, context, moved)
    return current[:, ::-1, ::-1, :]
```

```python
import functools
import math

import jax
import jax.numpy as jnp
from jax import lax
from jax.experimental import pallas as pl
from jax.experimental.pallas import tpu as pltpu
from jax.sharding import PartitionSpec as P

HD = 128
EPSILON = 1e-05
F32 = jnp.float32
BF16 = jnp.bfloat16


def split_bf16(value, pieces):
    out = []
    for _ in range(pieces):
        piece = value.astype(BF16)
        out.append(piece)
        value = value - piece.astype(F32)
    return out


def fold_kernel(embed_ref, qkv_ref, folded_ref, gram_ref, centred_ref):
    channels, width = embed_ref.shape

    @pl.when(pl.program_id(0) == 0)
    def _():
        rows = embed_ref[...].astype(F32)
        centred = rows - jnp.mean(rows, axis=1, keepdims=True)
        high, low = split_bf16(centred, 2)
        centred_ref[:channels] = high
        centred_ref[channels:] = low
        gram = lax.dot_general(
            centred, centred, (((1,), (1,)), ((), ())),
            precision=lax.Precision.HIGHEST, preferred_element_type=F32,
        ) * (1.0 / width)
        for index, piece in enumerate(split_bf16(gram, 3)):
            gram_ref[:, index * channels:(index + 1) * channels] = piece

    both = centred_ref[...]
    maps = []
    for index in range(3):
        product = jnp.dot(both, qkv_ref[index], preferred_element_type=F32)
        maps.append(product[:channels] + product[channels:])
    scale = math.log2(math.e) / math.sqrt(HD)
    heads = qkv_ref.shape[2] // HD
    folded_ref[0, channels:] = jnp.zeros((heads * HD, heads * HD), BF16)
    for head in range(heads):
        cols = slice(head * HD, (head + 1) * HD)
        score_map = lax.dot_general(
            maps[0][:, cols], maps[1][:, cols], (((1,), (1,)), ((), ())),
            precision=lax.Precision.HIGHEST, preferred_element_type=F32,
        ) * scale
        folded_ref[0, :channels, cols] = score_map.astype(BF16)
        folded_ref[0, channels + head * HD:channels + (head + 1) * HD, cols] = (
            maps[2][:, cols].astype(BF16)
        )


def fold_weights(w_embed, w_qkv):
    channels, width = w_embed.shape
    cols = w_qkv.shape[2]
    wide = 2 * HD
    pairs = cols // wide
    return pl.pallas_call(
        fold_kernel,
        grid=(pairs,),
        in_specs=[
            pl.BlockSpec((channels, width), lambda i: (0, 0)),
            pl.BlockSpec((3, width, wide), lambda i: (0, 0, i)),
        ],
        out_specs=[
            pl.BlockSpec((1, channels + wide, wide), lambda i: (i, 0, 0)),
            pl.BlockSpec((channels, 3 * channels), lambda i: (0, 0)),
        ],
        out_shape=[
            jax.ShapeDtypeStruct((pairs, channels + wide, wide), BF16),
            jax.ShapeDtypeStruct((channels, 3 * channels), BF16),
        ],
        scratch_shapes=[pltpu.VMEM((2 * channels, width), BF16)],
        cost_estimate=pl.CostEstimate(
            flops=4 * channels * width * 3 * cols, bytes_accessed=6 * width * cols, transcendentals=0
        ),
        name="fold",
    )(w_embed, w_qkv)


def flow_kernel(parts, place_ref, frozen_ref, read_ref, near_ref, far_ref, gram_ref, embed_hbm, head_hbm, *rest):
    folded_hbm, out_hbm = rest[:parts], rest[parts:2 * parts]
    (result_ref, raw, turned, valued, query_raw, query, keys, values, mapped, attended,
     folded, w_embed, w_out, w_head, sems) = rest[2 * parts:]
    half, tokens, channels = near_ref.shape
    frames = 2 * half
    links = read_ref.shape[1]
    slots = links + 1
    pairs_here = folded_hbm[0].shape[0]
    rows_here = out_hbm[0].shape[0]
    place = place_ref[0]

    loads = [
        pltpu.make_async_copy(embed_hbm, w_embed, sems.at[0]),
        pltpu.make_async_copy(head_hbm, w_head, sems.at[1]),
    ]
    folded_loads = []
    for part in range(parts):
        folded_loads.append(pltpu.make_async_copy(
            folded_hbm[part], folded.at[part * pairs_here:(part + 1) * pairs_here], sems.at[2 + part]))
        loads.append(pltpu.make_async_copy(
            out_hbm[part], w_out.at[part * rows_here:(part + 1) * rows_here], sems.at[2 + parts + part]))
    for load in folded_loads + loads:
        load.start()

    def slot_of(frame):
        shift = lax.rem(place // 2 - frame // 2 + half, half)
        return jnp.where(lax.rem(place + frame, 2) == 0, shift, half + shift)

    def ingest(slot, rounded):
        wide = rounded.astype(F32)
        spread = jnp.dot(rounded, gram_ref[...], preferred_element_type=F32)
        spread = spread[:, :channels] + spread[:, channels:2 * channels] + spread[:, 2 * channels:]
        variance = jnp.maximum(jnp.sum(spread * wide, axis=1, keepdims=True), 0.0)
        scaled = (wide * lax.rsqrt(variance + EPSILON)).astype(BF16)
        raw[slot] = rounded
        turned[slot] = scaled.T
        valued[slot, :, :channels] = scaled
        valued[slot, :, channels:] = jnp.ones((tokens, channels), BF16)

    def ingest_step(index, carry):
        ingest(index, near_ref[index])
        ingest(half + index, far_ref[index])
        return carry

    lax.fori_loop(0, half, ingest_step, 0)
    for load in folded_loads + loads:
        load.wait()

    target = frames - 1 - place
    last = target - 1
    last_safe = jnp.maximum(last, 0)
    run_all = jnp.logical_and(target > 0, frozen_ref[target] == 0)

    def flip():
        rows = lax.broadcasted_iota(jnp.int32, (tokens, tokens), 0)
        cols = lax.broadcasted_iota(jnp.int32, (tokens, tokens), 1)
        return jnp.where(rows + cols == tokens - 1, 1.0, 0.0).astype(BF16)

    def source_of(index):
        return jnp.where(index == 0, last_safe, read_ref[last_safe, jnp.maximum(index - 1, 0)])

    def is_run(index):
        frame = source_of(index)
        return jnp.logical_and(frame > 0, frozen_ref[jnp.maximum(frame, 0)] == 0)

    def attend():
        def head_pair(pair, carry):
            contexts = []
            for side in range(2):
                mapped_head = mapped[pair, :, side * HD:(side + 1) * HD]
                scores = jnp.dot(mapped_head, keys[...], preferred_element_type=F32)
                top = jnp.max(scores, axis=1, keepdims=True)
                weights = jnp.exp2(scores - top).astype(BF16)
                total = jnp.dot(weights, values[...], preferred_element_type=F32)
                contexts.append((total[:, :channels] / total[:, channels:]).astype(BF16))
            both = jnp.concatenate(contexts, axis=1)
            attended[:, pl.ds(pl.multiple_of(pair * 2 * HD, 2 * HD), 2 * HD)] = jnp.dot(
                both, folded[pair, channels:], preferred_element_type=F32
            ).astype(BF16)
            return carry

        lax.fori_loop(0, folded.shape[0], head_pair, 0)

    def evaluate():
        def map_pair(pair, carry):
            mapped[pair] = jnp.dot(
                query[...], folded[pair, :channels], preferred_element_type=F32
            ).astype(BF16)
            return carry

        lax.fori_loop(0, folded.shape[0], map_pair, 0)
        attend()
        residual = jnp.dot(query_raw[...], w_embed[...], preferred_element_type=F32) + jnp.dot(
            attended[...], w_out[...], preferred_element_type=F32
        )
        centred = residual - jnp.mean(residual, axis=1, keepdims=True)
        spread_sq = jnp.mean(centred * centred, axis=1, keepdims=True)
        head_in = (centred * lax.rsqrt(spread_sq + EPSILON)).astype(BF16)
        return jnp.dot(head_in, w_head[...], preferred_element_type=F32)

    def moved(held, predicted):
        return held * jnp.exp(jnp.tanh(predicted[:, channels:])) + predicted[:, :channels]

    def place_key(index, slot, usable):
        keys[:, index * tokens:(index + 1) * tokens] = turned[slot]
        block = valued[slot]
        values[index * tokens:(index + 1) * tokens] = jnp.where(usable, block, jnp.zeros_like(block))

    def round_step(step, carry):
        final = step == slots

        @pl.when(jnp.logical_and(run_all, jnp.logical_or(final, is_run(jnp.minimum(step, slots - 1)))))
        def _():
            frame = jnp.where(final, last_safe, source_of(jnp.minimum(step, slots - 1)) - 1)
            frame = jnp.maximum(frame, 0)
            own = jnp.where(jnp.logical_and(final, is_run(0)), frames, slot_of(frame))
            query_raw[...] = raw[own]
            query[...] = valued[own, :, :channels]
            place_key(0, own, True)
            for link in range(links):
                source = read_ref[frame, link]
                usable = source >= 0
                held = slot_of(jnp.maximum(source, 0))
                held = jnp.where(jnp.logical_and(final, is_run(link + 1)), frames + link + 1, held)
                place_key(link + 1, jnp.where(usable, held, own), usable)

            @pl.when(final)
            def _():
                mirror = flip()
                query_raw[...] = jnp.dot(mirror, query_raw[...], preferred_element_type=F32).astype(BF16)
                query[...] = jnp.dot(mirror, query[...], preferred_element_type=F32).astype(BF16)

            predicted = evaluate()

            @pl.when(jnp.logical_not(final))
            def _():
                base = raw[slot_of(frame + 1)].astype(F32)
                ingest(frames + step, moved(base, predicted).astype(BF16))

            @pl.when(final)
            def _():
                base = jnp.dot(flip(), raw[slot_of(target)], preferred_element_type=F32)
                result_ref[...] = moved(base, predicted)

        return carry

    lax.fori_loop(0, slots + 1, round_step, 0)

    @pl.when(jnp.logical_not(run_all))
    def _():
        result_ref[...] = jnp.dot(flip(), raw[slot_of(target)], preferred_element_type=F32)


def run_flow(place, frozen, read_list, near, far, gram, w_embed, w_head, folded, outs):
    half, tokens, channels = near.shape
    frames = 2 * half
    parts = len(folded)
    slots = read_list.shape[1] + 1
    width = w_embed.shape[1]
    pairs = sum(block.shape[0] for block in folded)
    hidden = sum(block.shape[0] for block in outs)
    vmem = pl.BlockSpec(memory_space=pltpu.VMEM)
    smem = pl.BlockSpec(memory_space=pltpu.SMEM)
    anywhere = pl.BlockSpec(memory_space=pl.ANY)
    held = frames + slots
    return pl.pallas_call(
        functools.partial(flow_kernel, parts),
        in_specs=[smem, smem, smem, vmem, vmem, vmem, anywhere, anywhere] + [anywhere] * (2 * parts),
        out_specs=vmem,
        out_shape=jax.ShapeDtypeStruct((tokens, channels), F32),
        scratch_shapes=[
            pltpu.VMEM((held, tokens, channels), BF16),
            pltpu.VMEM((held, channels, tokens), BF16),
            pltpu.VMEM((held, tokens, 2 * channels), BF16),
            pltpu.VMEM((tokens, channels), BF16),
            pltpu.VMEM((tokens, channels), BF16),
            pltpu.VMEM((channels, slots * tokens), BF16),
            pltpu.VMEM((slots * tokens, 2 * channels), BF16),
            pltpu.VMEM((pairs, tokens, 2 * HD), BF16),
            pltpu.VMEM((tokens, hidden), BF16),
            pltpu.VMEM((pairs,) + folded[0].shape[1:], BF16),
            pltpu.VMEM(w_embed.shape, BF16),
            pltpu.VMEM((hidden, width), BF16),
            pltpu.VMEM(w_head.shape, BF16),
            pltpu.SemaphoreType.DMA((2 + 2 * parts,)),
        ],
        compiler_params=pltpu.CompilerParams(vmem_limit_bytes=56 * 1024 * 1024),
        name="flow",
    )(place, frozen, read_list, near, far, gram, w_embed, w_head, *folded, *outs)


def from_behind(value, axis, shift):
    count = lax.axis_size(axis)
    return lax.ppermute(value, axis, [(source, (source + shift) % count) for source in range(count)])


def per_device(latent, context, frozen, read_list, w_embed, w_qkv, w_attn_out, w_head):
    position = lax.axis_index("seq")
    seq_count = lax.axis_size("seq")
    clip_count = lax.axis_size("clip")
    layout = latent.shape
    frozen_here = lax.dynamic_index_in_dim(frozen, position, 0, keepdims=False) == 1
    held = jnp.where(frozen_here, context, latent).astype(BF16).reshape(layout[-2], layout[-1])
    shifted = [held] + [from_behind(held, "seq", 2 * step) for step in range(1, seq_count // 2)]
    near = jnp.stack(shifted)
    far = lax.ppermute(near, "seq", [(source, source ^ 1) for source in range(seq_count)])
    outs = [w_attn_out] + [from_behind(w_attn_out, "clip", step) for step in range(1, clip_count)]
    folded, gram = fold_weights(w_embed, w_qkv)
    folded = [folded] + [from_behind(folded, "clip", step) for step in range(1, clip_count)]
    result = run_flow(
        position.reshape(1).astype(jnp.int32), frozen, read_list, near, far, gram, w_embed, w_head, folded, outs
    )
    return result.reshape(layout)


def solution(mesh):
    return jax.shard_map(
        per_device,
        mesh=mesh,
        in_specs=(
            P(("group", "clip"), "seq", None, None),
            P(("group", "clip"), "seq", None, None),
            P("group"),
            P("group", None),
            P(),
            P(None, None, "clip"),
            P("clip", None),
            P(),
        ),
        out_specs=P(("group", "clip"), "seq", None, None),
        check_vma=False,
    )
```

```python
import functools
import math

import jax
import jax.numpy as jnp
from jax import lax
from jax.experimental import pallas as pl
from jax.experimental.pallas import tpu as pltpu
from jax.sharding import PartitionSpec as P

HD = 128
EPSILON = 1e-05
F32 = jnp.float32
BF16 = jnp.bfloat16


def split_bf16(value, pieces):
    out = []
    for _ in range(pieces):
        piece = value.astype(BF16)
        out.append(piece)
        value = value - piece.astype(F32)
    return out


def fold_kernel(embed_ref, qkv_ref, folded_ref, gram_ref, centred_ref):
    channels, width = embed_ref.shape

    @pl.when(pl.program_id(0) == 0)
    def _():
        rows = embed_ref[...].astype(F32)
        centred = rows - jnp.mean(rows, axis=1, keepdims=True)
        high, low = split_bf16(centred, 2)
        centred_ref[:channels] = high
        centred_ref[channels:] = low
        gram = lax.dot_general(
            centred, centred, (((1,), (1,)), ((), ())),
            precision=lax.Precision.HIGHEST, preferred_element_type=F32,
        ) * (1.0 / width)
        for index, piece in enumerate(split_bf16(gram, 3)):
            gram_ref[:, index * channels:(index + 1) * channels] = piece

    both = centred_ref[...]
    maps = []
    for index in range(3):
        product = jnp.dot(both, qkv_ref[index], preferred_element_type=F32)
        maps.append(product[:channels] + product[channels:])
    scale = math.log2(math.e) / math.sqrt(HD)
    heads = qkv_ref.shape[2] // HD
    folded_ref[0, :, channels:] = jnp.zeros((heads * HD, heads * HD), BF16)
    for head in range(heads):
        cols = slice(head * HD, (head + 1) * HD)
        score_map = lax.dot_general(
            maps[1][:, cols], maps[0][:, cols], (((1,), (1,)), ((), ())),
            precision=lax.Precision.HIGHEST, preferred_element_type=F32,
        ) * scale
        folded_ref[0, cols, :channels] = score_map.astype(BF16)
        folded_ref[0, cols, channels + head * HD:channels + (head + 1) * HD] = (
            maps[2][:, cols].T.astype(BF16)
        )


def fold_weights(w_embed, w_qkv):
    channels, width = w_embed.shape
    cols = w_qkv.shape[2]
    wide = 2 * HD
    pairs = cols // wide
    return pl.pallas_call(
        fold_kernel,
        grid=(pairs,),
        in_specs=[
            pl.BlockSpec((channels, width), lambda i: (0, 0)),
            pl.BlockSpec((3, width, wide), lambda i: (0, 0, i)),
        ],
        out_specs=[
            pl.BlockSpec((1, wide, channels + wide), lambda i: (i, 0, 0)),
            pl.BlockSpec((channels, 3 * channels), lambda i: (0, 0)),
        ],
        out_shape=[
            jax.ShapeDtypeStruct((pairs, wide, channels + wide), BF16),
            jax.ShapeDtypeStruct((channels, 3 * channels), BF16),
        ],
        scratch_shapes=[pltpu.VMEM((2 * channels, width), BF16)],
        cost_estimate=pl.CostEstimate(
            flops=4 * channels * width * 3 * cols, bytes_accessed=6 * width * cols, transcendentals=0
        ),
        name="fold",
    )(w_embed, w_qkv)


def flow_kernel(parts, place_ref, frozen_ref, read_ref, near_ref, far_ref, gram_ref, embed_hbm, head_hbm, *rest):
    folded_hbm, out_hbm = rest[:parts], rest[parts:2 * parts]
    (result_ref, raw, turned, straight, query_raw, query, keys, values, mapped, attended,
     folded, w_embed, w_out, w_head, sems) = rest[2 * parts:]
    half, tokens, channels = near_ref.shape
    frames = 2 * half
    links = read_ref.shape[1]
    slots = links + 1
    pairs_here = folded_hbm[0].shape[0]
    rows_here = out_hbm[0].shape[0]
    place = place_ref[0]

    loads = [
        pltpu.make_async_copy(embed_hbm, w_embed, sems.at[0]),
        pltpu.make_async_copy(head_hbm, w_head, sems.at[1]),
    ]
    folded_loads = []
    for part in range(parts):
        folded_loads.append(pltpu.make_async_copy(
            folded_hbm[part], folded.at[part * pairs_here:(part + 1) * pairs_here], sems.at[2 + part]))
        loads.append(pltpu.make_async_copy(
            out_hbm[part], w_out.at[part * rows_here:(part + 1) * rows_here], sems.at[2 + parts + part]))
    for load in folded_loads + loads:
        load.start()

    def slot_of(frame):
        shift = lax.rem(place // 2 - frame // 2 + half, half)
        return jnp.where(lax.rem(place + frame, 2) == 0, shift, half + shift)

    def ingest(slot, rounded):
        wide = rounded.astype(F32)
        spread = jnp.dot(rounded, gram_ref[...], preferred_element_type=F32)
        spread = spread[:, :channels] + spread[:, channels:2 * channels] + spread[:, 2 * channels:]
        variance = jnp.maximum(jnp.sum(spread * wide, axis=1, keepdims=True), 0.0)
        scaled = (wide * lax.rsqrt(variance + EPSILON)).astype(BF16)
        raw[slot] = rounded
        straight[slot] = scaled
        turned[slot, :channels] = scaled.T
        turned[slot, channels:] = jnp.ones((turned.shape[1] - channels, tokens), BF16)

    def ingest_step(index, carry):
        ingest(index, near_ref[index])
        ingest(half + index, far_ref[index])
        return carry

    lax.fori_loop(0, half, ingest_step, 0)
    for load in folded_loads + loads:
        load.wait()

    target = frames - 1 - place
    last = target - 1
    last_safe = jnp.maximum(last, 0)
    run_all = jnp.logical_and(target > 0, frozen_ref[target] == 0)

    def flip():
        rows = lax.broadcasted_iota(jnp.int32, (tokens, tokens), 0)
        cols = lax.broadcasted_iota(jnp.int32, (tokens, tokens), 1)
        return jnp.where(rows + cols == tokens - 1, 1.0, 0.0).astype(BF16)

    def source_of(index):
        return jnp.where(index == 0, last_safe, read_ref[last_safe, jnp.maximum(index - 1, 0)])

    def is_run(index):
        frame = source_of(index)
        return jnp.logical_and(frame > 0, frozen_ref[jnp.maximum(frame, 0)] == 0)

    def attend():
        heads = 2 * folded.shape[0]

        def scores_of(head):
            return jnp.dot(
                keys[...], mapped[head // 2, (head % 2) * HD:(head % 2 + 1) * HD], preferred_element_type=F32
            )

        def context_of(scores):
            weights = jnp.exp2(scores - jnp.max(scores, axis=0, keepdims=True)).astype(BF16)
            total = jnp.dot(values[...], weights, preferred_element_type=F32)
            return (total[:channels] / total[channels:channels + 1]).astype(BF16)

        scores, contexts = scores_of(0), []
        for head in range(heads):
            following = scores_of(head + 1) if head + 1 < heads else None
            contexts.append(context_of(scores))
            scores = following
            if head % 2:
                pair = head // 2
                mixed = jnp.dot(
                    folded[pair, :, channels:], jnp.concatenate(contexts, axis=0), preferred_element_type=F32
                )
                attended[:, pair * 2 * HD:(pair + 1) * 2 * HD] = mixed.astype(BF16).T
                contexts = []

    def evaluate():
        for pair in range(folded.shape[0]):
            mapped[pair] = jnp.dot(
                folded[pair, :, :channels], query[...], preferred_element_type=F32
            ).astype(BF16)
        attend()
        residual = jnp.dot(query_raw[...], w_embed[...], preferred_element_type=F32) + jnp.dot(
            attended[...], w_out[...], preferred_element_type=F32
        )
        centred = residual - jnp.mean(residual, axis=1, keepdims=True)
        spread_sq = jnp.mean(centred * centred, axis=1, keepdims=True)
        head_in = (centred * lax.rsqrt(spread_sq + EPSILON)).astype(BF16)
        return jnp.dot(head_in, w_head[...], preferred_element_type=F32)

    def moved(held, predicted):
        return held * jnp.exp(jnp.tanh(predicted[:, channels:])) + predicted[:, :channels]

    def place_key(index, slot, usable):
        keys[index * tokens:(index + 1) * tokens] = straight[slot]
        block = turned[slot]
        values[:, index * tokens:(index + 1) * tokens] = jnp.where(usable, block, jnp.zeros_like(block))

    def round_step(step, carry):
        final = step == slots

        @pl.when(jnp.logical_and(run_all, jnp.logical_or(final, is_run(jnp.minimum(step, slots - 1)))))
        def _():
            frame = jnp.where(final, last_safe, source_of(jnp.minimum(step, slots - 1)) - 1)
            frame = jnp.maximum(frame, 0)
            own = jnp.where(jnp.logical_and(final, is_run(0)), frames, slot_of(frame))
            query_raw[...] = raw[own]
            query[...] = turned[own, :channels]
            place_key(0, own, True)
            for link in range(links):
                source = read_ref[frame, link]
                usable = source >= 0
                held = slot_of(jnp.maximum(source, 0))
                held = jnp.where(jnp.logical_and(final, is_run(link + 1)), frames + link + 1, held)
                place_key(link + 1, jnp.where(usable, held, own), usable)

            @pl.when(final)
            def _():
                mirror = flip()
                query_raw[...] = jnp.dot(mirror, query_raw[...], preferred_element_type=F32).astype(BF16)
                query[...] = jnp.dot(query[...], mirror, preferred_element_type=F32).astype(BF16)

            predicted = evaluate()

            @pl.when(jnp.logical_not(final))
            def _():
                base = raw[slot_of(frame + 1)].astype(F32)
                ingest(frames + step, moved(base, predicted).astype(BF16))

            @pl.when(final)
            def _():
                base = jnp.dot(flip(), raw[slot_of(target)], preferred_element_type=F32)
                result_ref[...] = moved(base, predicted)

        return carry

    lax.fori_loop(0, slots + 1, round_step, 0)

    @pl.when(jnp.logical_not(run_all))
    def _():
        result_ref[...] = jnp.dot(flip(), raw[slot_of(target)], preferred_element_type=F32)


def run_flow(place, frozen, read_list, near, far, gram, w_embed, w_head, folded, outs):
    half, tokens, channels = near.shape
    frames = 2 * half
    parts = len(folded)
    slots = read_list.shape[1] + 1
    width = w_embed.shape[1]
    pairs = sum(block.shape[0] for block in folded)
    hidden = sum(block.shape[0] for block in outs)
    vmem = pl.BlockSpec(memory_space=pltpu.VMEM)
    smem = pl.BlockSpec(memory_space=pltpu.SMEM)
    anywhere = pl.BlockSpec(memory_space=pl.ANY)
    held = frames + slots
    return pl.pallas_call(
        functools.partial(flow_kernel, parts),
        in_specs=[smem, smem, smem, vmem, vmem, vmem, anywhere, anywhere] + [anywhere] * (2 * parts),
        out_specs=vmem,
        out_shape=jax.ShapeDtypeStruct((tokens, channels), F32),
        scratch_shapes=[
            pltpu.VMEM((held, tokens, channels), BF16),
            pltpu.VMEM((held, channels + 16, tokens), BF16),
            pltpu.VMEM((held, tokens, channels), BF16),
            pltpu.VMEM((tokens, channels), BF16),
            pltpu.VMEM((channels, tokens), BF16),
            pltpu.VMEM((slots * tokens, channels), BF16),
            pltpu.VMEM((channels + 16, slots * tokens), BF16),
            pltpu.VMEM((pairs, 2 * HD, tokens), BF16),
            pltpu.VMEM((tokens, hidden), BF16),
            pltpu.VMEM((pairs,) + folded[0].shape[1:], BF16),
            pltpu.VMEM(w_embed.shape, BF16),
            pltpu.VMEM((hidden, width), BF16),
            pltpu.VMEM(w_head.shape, BF16),
            pltpu.SemaphoreType.DMA((2 + 2 * parts,)),
        ],
        compiler_params=pltpu.CompilerParams(vmem_limit_bytes=56 * 1024 * 1024),
        name="flow",
    )(place, frozen, read_list, near, far, gram, w_embed, w_head, *folded, *outs)


def from_behind(value, axis, shift):
    count = lax.axis_size(axis)
    return lax.ppermute(value, axis, [(source, (source + shift) % count) for source in range(count)])


def per_device(latent, context, frozen, read_list, w_embed, w_qkv, w_attn_out, w_head):
    position = lax.axis_index("seq")
    seq_count = lax.axis_size("seq")
    clip_count = lax.axis_size("clip")
    layout = latent.shape
    frozen_here = lax.dynamic_index_in_dim(frozen, position, 0, keepdims=False) == 1
    held = jnp.where(frozen_here, context, latent).astype(BF16).reshape(layout[-2], layout[-1])
    shifted = [held] + [from_behind(held, "seq", 2 * step) for step in range(1, seq_count // 2)]
    near = jnp.stack(shifted)
    far = lax.ppermute(near, "seq", [(source, source ^ 1) for source in range(seq_count)])
    outs = [w_attn_out] + [from_behind(w_attn_out, "clip", step) for step in range(1, clip_count)]
    folded, gram = fold_weights(w_embed, w_qkv)
    folded = [folded] + [from_behind(folded, "clip", step) for step in range(1, clip_count)]
    result = run_flow(
        position.reshape(1).astype(jnp.int32), frozen, read_list, near, far, gram, w_embed, w_head, folded, outs
    )
    return result.reshape(layout)


def solution(mesh):
    return jax.shard_map(
        per_device,
        mesh=mesh,
        in_specs=(
            P(("group", "clip"), "seq", None, None),
            P(("group", "clip"), "seq", None, None),
            P("group"),
            P("group", None),
            P(),
            P(None, None, "clip"),
            P("clip", None),
            P(),
        ),
        out_specs=P(("group", "clip"), "seq", None, None),
        check_vma=False,
    )
```

```python
import functools
import math

import jax
import jax.numpy as jnp
from jax import lax
from jax.experimental import pallas as pl
from jax.experimental.pallas import tpu as pltpu
from jax.sharding import PartitionSpec as P


HD = 128
EPSILON = 1e-05
F32 = jnp.float32
BF16 = jnp.bfloat16


def split_bf16(value, pieces):
    out = []
    for _ in range(pieces):
        piece = value.astype(BF16)
        out.append(piece)
        value = value - piece.astype(F32)
    return out


def fold_kernel(embed_ref, qkv_hbm, folded_ref, gram_ref, qkv, centred_ref, sems):
    channels, width = embed_ref.shape
    pairs = folded_ref.shape[0]
    loads = [pltpu.make_async_copy(qkv_hbm.at[index], qkv.at[index], sems.at[index]) for index in range(3)]
    for load in loads:
        load.start()

    rows = embed_ref[...].astype(F32)
    centred = rows - jnp.mean(rows, axis=1, keepdims=True)
    high, low = split_bf16(centred, 2)
    centred_ref[:channels] = high
    centred_ref[channels:] = low
    square = lax.dot_general(
        centred_ref[...], centred_ref[...], (((1,), (1,)), ((), ())), preferred_element_type=F32
    )
    gram = (
        square[:channels, :channels] + square[channels:, channels:]
        + square[:channels, channels:] + square[channels:, :channels]
    ) * (1.0 / width)
    for index, piece in enumerate(split_bf16(gram, 3)):
        gram_ref[:, index * channels:(index + 1) * channels] = piece

    scale = math.log2(math.e) / math.sqrt(HD)
    maps = []
    for index in range(3):
        loads[index].wait()
        product = jnp.dot(centred_ref[...], qkv[index], preferred_element_type=F32)
        maps.append(product[:channels] + product[channels:])
        if index == 1:
            for head in range(2 * pairs):
                cols = slice(head * HD, (head + 1) * HD)
                queries = split_bf16(maps[0][:, cols] * scale, 2)
                keys = split_bf16(maps[1][:, cols], 2)
                score_map = lax.dot_general(
                    jnp.concatenate([keys[0], keys[0]], axis=1), jnp.concatenate(queries, axis=1),
                    (((1,), (1,)), ((), ())), preferred_element_type=F32,
                ) + lax.dot_general(
                    keys[1], queries[0], (((1,), (1,)), ((), ())), preferred_element_type=F32
                )
                half = head % 2 * HD
                folded_ref[head // 2, half:half + HD, :channels] = score_map.astype(BF16)
    for head in range(2 * pairs):
        half = head % 2 * HD
        mixed = maps[2][:, head * HD:(head + 1) * HD].T.astype(BF16)
        blank = jnp.zeros((HD, channels), BF16)
        folded_ref[head // 2, half:half + HD, channels:] = jnp.concatenate(
            [blank, mixed] if head % 2 else [mixed, blank], axis=1
        )


def fold_weights(w_embed, w_qkv):
    channels, width = w_embed.shape
    cols = w_qkv.shape[2]
    wide = 2 * HD
    pairs = cols // wide
    vmem = pl.BlockSpec(memory_space=pltpu.VMEM)
    return pl.pallas_call(
        fold_kernel,
        in_specs=[vmem, pl.BlockSpec(memory_space=pl.ANY)],
        out_specs=[vmem, vmem],
        out_shape=[
            jax.ShapeDtypeStruct((pairs, wide, channels + wide), BF16),
            jax.ShapeDtypeStruct((channels, 3 * channels), BF16),
        ],
        scratch_shapes=[
            pltpu.VMEM((3, width, cols), BF16),
            pltpu.VMEM((2 * channels, width), BF16),
            pltpu.SemaphoreType.DMA((3,)),
        ],
        compiler_params=pltpu.CompilerParams(vmem_limit_bytes=67043328),
        cost_estimate=pl.CostEstimate(
            flops=4 * channels * width * 3 * cols, bytes_accessed=6 * width * cols, transcendentals=0
        ),
        name="fold",
    )(w_embed, w_qkv)


def flow_kernel(counts, place_ref, frozen_ref, read_ref, gram_hbm, embed_hbm, head_hbm, *rest):
    frames, parts = counts
    block_hbm, rest = rest[:frames], rest[frames:]
    folded_hbm, out_hbm, rest = rest[:parts], rest[parts:2 * parts], rest[2 * parts:]
    (result_ref, raw, turned, straight, query, keys, values, mapped, attended,
     folded, w_out, w_head, gram_ref, ready, sems) = rest
    tokens, channels = raw.shape[1:]
    links = read_ref.shape[0]
    slots = links + 1
    pairs_here = folded_hbm[0].shape[0]
    rows_here = out_hbm[0].shape[0]
    hidden = parts * rows_here
    place = place_ref[0]

    block_loads = [
        pltpu.make_async_copy(block_hbm[slot], raw.at[slot], sems.at[slot]) for slot in range(frames)
    ]
    block_loads.append(pltpu.make_async_copy(gram_hbm, gram_ref, sems.at[frames + 2 * parts + 2]))
    folded_loads, late_loads = [], []
    for part in range(parts):
        folded_loads.append(pltpu.make_async_copy(
            folded_hbm[part], folded.at[part * pairs_here:(part + 1) * pairs_here], sems.at[frames + part]))
        late_loads.append(pltpu.make_async_copy(
            out_hbm[part], w_out.at[part * rows_here:(part + 1) * rows_here], sems.at[frames + parts + part]))
    late_loads.append(pltpu.make_async_copy(embed_hbm, w_out.at[hidden:], sems.at[frames + 2 * parts]))
    late_loads.append(pltpu.make_async_copy(head_hbm, w_head, sems.at[frames + 2 * parts + 1]))
    for load in block_loads + folded_loads + late_loads:
        load.start()
    ready[0] = 0

    def await_late():
        @pl.when(ready[0] == 0)
        def _():
            for load in late_loads:
                load.wait()
            ready[0] = 1

    def slot_of(frame):
        return jnp.bitwise_xor(place, frame)

    def ingest(slot, rounded):
        wide = rounded.astype(F32)
        spread = jnp.dot(rounded, gram_ref[...], preferred_element_type=F32)
        spread = spread[:, :channels] + spread[:, channels:2 * channels] + spread[:, 2 * channels:]
        variance = jnp.maximum(jnp.sum(spread * wide, axis=1, keepdims=True), 0.0)
        scaled = (wide * lax.rsqrt(variance + EPSILON)).astype(BF16)
        straight[slot] = scaled
        turned[slot, :channels] = scaled.T
        turned[slot, channels:] = jnp.ones((turned.shape[1] - channels, tokens), BF16)

    for load in block_loads:
        load.wait()
    group = math.gcd(frames, 4)

    def ingest_step(index, carry):
        for side in range(group):
            slot = index * group + side
            ingest(slot, raw[slot])
        return carry

    lax.fori_loop(0, frames // group, ingest_step, 0)
    for load in folded_loads:
        load.wait()

    target = frames - 1 - place
    last = target - 1
    last_safe = jnp.maximum(last, 0)
    run_all = jnp.logical_and(target > 0, frozen_ref[target] == 0)

    def flip():
        rows = lax.broadcasted_iota(jnp.int32, (tokens, tokens), 0)
        cols = lax.broadcasted_iota(jnp.int32, (tokens, tokens), 1)
        return jnp.where(rows + cols == tokens - 1, 1.0, 0.0).astype(BF16)

    def source_of(index):
        return jnp.where(index == 0, last_safe, read_ref[jnp.maximum(index - 1, 0), last_safe])

    def is_run(index):
        frame = source_of(index)
        return jnp.logical_and(frame > 0, frozen_ref[jnp.maximum(frame, 0)] == 0)

    def scores_of(pair, side):
        return jnp.dot(keys[...], mapped[pair, side * HD:(side + 1) * HD], preferred_element_type=F32)

    def context_of(exponents):
        weights = jnp.exp2(exponents).astype(BF16)
        total = jnp.dot(values[...], weights, preferred_element_type=F32)
        mass = total[channels:channels + 1]
        return (total[:channels] / mass).astype(BF16), mass

    def mix(pair, contexts):
        mixed = jnp.dot(
            folded[pair, :, channels:], jnp.concatenate(contexts, axis=0), preferred_element_type=F32
        )
        return mixed.astype(BF16).T

    def attend():
        heads = 2 * folded.shape[0]
        scores, contexts = scores_of(0, 0), []
        fits = jnp.ones((1, tokens), F32)
        for head in range(heads):
            following = scores_of((head + 1) // 2, (head + 1) % 2) if head + 1 < heads else None
            context, mass = context_of(scores)
            fits = jnp.where(jnp.logical_and(mass > 2.0 ** -80, mass < 2.0 ** 110), fits, 0.0)
            contexts.append(context)
            scores = following
            if head % 2:
                pair = head // 2
                attended[:, pair * 2 * HD:(pair + 1) * 2 * HD] = mix(pair, contexts)
                contexts = []

        @pl.when(jnp.min(fits) < 0.5)
        def _():
            def shifted_pair(pair, carry):
                contexts = []
                for side in range(2):
                    scores = scores_of(pair, side)
                    contexts.append(context_of(scores - jnp.max(scores, axis=0, keepdims=True))[0])
                start = pl.multiple_of(pair * 2 * HD, 2 * HD)
                attended[:, pl.ds(start, 2 * HD)] = mix(pair, contexts)
                return carry

            lax.fori_loop(0, folded.shape[0], shifted_pair, 0)

    def evaluate():
        for pair in range(folded.shape[0]):
            mapped[pair] = jnp.dot(
                folded[pair, :, :channels], query[...], preferred_element_type=F32
            ).astype(BF16)
        attend()
        await_late()
        residual = jnp.dot(attended[...], w_out[...], preferred_element_type=F32)
        centred = residual - jnp.mean(residual, axis=1, keepdims=True)
        spread_sq = jnp.mean(centred * centred, axis=1, keepdims=True)
        head_in = (centred * lax.rsqrt(spread_sq + EPSILON)).astype(BF16)
        return jnp.dot(head_in, w_head[...], preferred_element_type=F32)

    def moved(held, predicted):
        return held * jnp.exp(jnp.tanh(predicted[:, channels:])) + predicted[:, :channels]

    def place_key(index, slot, usable):
        keys[index * tokens:(index + 1) * tokens] = straight[slot]
        block = turned[slot]
        values[:, index * tokens:(index + 1) * tokens] = jnp.where(usable, block, jnp.zeros_like(block))

    def round_step(step, carry):
        final = step == slots

        @pl.when(jnp.logical_and(run_all, jnp.logical_or(final, is_run(jnp.minimum(step, slots - 1)))))
        def _():
            frame = jnp.where(final, last_safe, source_of(jnp.minimum(step, slots - 1)) - 1)
            frame = jnp.maximum(frame, 0)
            own = jnp.where(jnp.logical_and(final, is_run(0)), frames, slot_of(frame))
            attended[:, hidden:] = raw[own]
            query[...] = turned[own, :channels]
            place_key(0, own, True)
            for link in range(links):
                source = read_ref[link, frame]
                usable = source >= 0
                held = slot_of(jnp.maximum(source, 0))
                held = jnp.where(jnp.logical_and(final, is_run(link + 1)), frames + link + 1, held)
                place_key(link + 1, jnp.where(usable, held, own), usable)

            @pl.when(final)
            def _():
                mirror = flip()
                attended[:, hidden:] = jnp.dot(mirror, raw[own], preferred_element_type=F32).astype(BF16)
                query[...] = jnp.dot(query[...], mirror, preferred_element_type=F32).astype(BF16)

            predicted = evaluate()

            @pl.when(jnp.logical_not(final))
            def _():
                base = raw[slot_of(frame + 1)].astype(F32)
                rounded = moved(base, predicted).astype(BF16)
                raw[frames + step] = rounded
                ingest(frames + step, rounded)

            @pl.when(final)
            def _():
                base = jnp.dot(flip(), raw[slot_of(target)], preferred_element_type=F32)
                result_ref[...] = moved(base, predicted)

        return carry

    lax.fori_loop(0, slots + 1, round_step, 0)
    await_late()

    @pl.when(jnp.logical_not(run_all))
    def _():
        result_ref[...] = jnp.dot(flip(), raw[slot_of(target)], preferred_element_type=F32)


def run_flow(place, frozen, read_list, blocks, gram, w_embed, w_head, folded, outs):
    tokens, channels = blocks[0].shape
    frames = len(blocks)
    parts = len(folded)
    slots = read_list.shape[0] + 1
    width = w_embed.shape[1]
    pairs = sum(block.shape[0] for block in folded)
    hidden = sum(block.shape[0] for block in outs)
    vmem = pl.BlockSpec(memory_space=pltpu.VMEM)
    smem = pl.BlockSpec(memory_space=pltpu.SMEM)
    anywhere = pl.BlockSpec(memory_space=pl.ANY)
    held = frames + slots
    return pl.pallas_call(
        functools.partial(flow_kernel, (frames, parts)),
        in_specs=[smem, smem, smem] + [anywhere] * (3 + frames + 2 * parts),
        out_specs=vmem,
        out_shape=jax.ShapeDtypeStruct((tokens, channels), F32),
        scratch_shapes=[
            pltpu.VMEM((held, tokens, channels), BF16),
            pltpu.VMEM((held, channels + 16, tokens), BF16),
            pltpu.VMEM((held, tokens, channels), BF16),
            pltpu.VMEM((channels, tokens), BF16),
            pltpu.VMEM((slots * tokens, channels), BF16),
            pltpu.VMEM((channels + 16, slots * tokens), BF16),
            pltpu.VMEM((pairs, 2 * HD, tokens), BF16),
            pltpu.VMEM((tokens, hidden + channels), BF16),
            pltpu.VMEM((pairs,) + folded[0].shape[1:], BF16),
            pltpu.VMEM((hidden + channels, width), BF16),
            pltpu.VMEM(w_head.shape, BF16),
            pltpu.VMEM(gram.shape, BF16),
            pltpu.SMEM((1,), jnp.int32),
            pltpu.SemaphoreType.DMA((frames + 3 + 2 * parts,)),
        ],
        compiler_params=pltpu.CompilerParams(vmem_limit_bytes=67043328),
        name="flow",
    )(place, frozen, read_list, gram, w_embed, w_head, *blocks, *folded, *outs)


def from_behind(value, axis, shift):
    count = lax.axis_size(axis)
    return lax.ppermute(value, axis, [(source, (source + shift) % count) for source in range(count)])


def across(value, axis, mask):
    return lax.ppermute(value, axis, [(source, source ^ mask) for source in range(lax.axis_size(axis))])


def per_device(latent, context, frozen, read_list, w_embed, w_qkv, w_attn_out, w_head):
    position = lax.axis_index("seq")
    seq_count = lax.axis_size("seq")
    clip_count = lax.axis_size("clip")
    layout = latent.shape
    frozen_here = lax.dynamic_index_in_dim(frozen, position, 0, keepdims=False) == 1
    held = jnp.where(frozen_here, context, latent).astype(BF16).reshape(layout[-2], layout[-1])
    blocks = [None] * seq_count
    blocks[0] = held
    for mask in [1] + list(range(2, seq_count, 2)):
        blocks[mask] = across(held, "seq", mask)
    for mask in range(2, seq_count, 2):
        blocks[mask + 1] = across(blocks[mask], "seq", 1)
    outs = [w_attn_out] + [from_behind(w_attn_out, "clip", step) for step in range(1, clip_count)]
    folded, gram = fold_weights(w_embed, w_qkv)
    folded = [folded] + [from_behind(folded, "clip", step) for step in range(1, clip_count)]
    result = run_flow(
        position.reshape(1).astype(jnp.int32), frozen, read_list.T, blocks, gram, w_embed, w_head, folded, outs
    )
    return result.reshape(layout)


def solution(mesh):
    return jax.shard_map(
        per_device,
        mesh=mesh,
        in_specs=(
            P(("group", "clip"), "seq", None, None),
            P(("group", "clip"), "seq", None, None),
            P("group"),
            P("group", None),
            P(),
            P(None, None, "clip"),
            P("clip", None),
            P(),
        ),
        out_specs=P(("group", "clip"), "seq", None, None),
        check_vma=False,
    )
```

```python
import functools
import math

import jax
import jax.numpy as jnp
from jax import lax
from jax.experimental import pallas as pl
from jax.experimental.pallas import tpu as pltpu
from jax.sharding import PartitionSpec as P


HD = 128
EPSILON = 1e-05
F32 = jnp.float32
BF16 = jnp.bfloat16


def split_bf16(value, pieces):
    out = []
    for _ in range(pieces):
        piece = value.astype(BF16)
        out.append(piece)
        value = value - piece.astype(F32)
    return out


def fold_kernel(embed_ref, qkv_ref, folded_ref, gram_ref, centred_ref):
    channels, width = embed_ref.shape
    pairs = folded_ref.shape[0]
    rows = embed_ref[...].astype(F32)
    centred = rows - jnp.mean(rows, axis=1, keepdims=True)
    high, low = split_bf16(centred, 2)
    centred_ref[:channels] = high
    centred_ref[channels:] = low
    square = lax.dot_general(
        centred_ref[...], centred_ref[...], (((1,), (1,)), ((), ())), preferred_element_type=F32
    )
    gram = (
        square[:channels, :channels] + square[channels:, channels:]
        + square[:channels, channels:] + square[channels:, :channels]
    ) * (1.0 / width)
    for index, piece in enumerate(split_bf16(gram, 3)):
        gram_ref[:, index * channels:(index + 1) * channels] = piece

    scale = math.log2(math.e) / math.sqrt(HD)
    maps = []
    for index in range(3):
        product = jnp.dot(centred_ref[...], qkv_ref[index], preferred_element_type=F32)
        maps.append(product[:channels] + product[channels:])
        if index == 1:
            for head in range(2 * pairs):
                cols = slice(head * HD, (head + 1) * HD)
                queries = split_bf16(maps[0][:, cols] * scale, 2)
                keys = split_bf16(maps[1][:, cols], 2)
                score_map = lax.dot_general(
                    jnp.concatenate([keys[0], keys[0]], axis=1), jnp.concatenate(queries, axis=1),
                    (((1,), (1,)), ((), ())), preferred_element_type=F32,
                ) + lax.dot_general(
                    keys[1], queries[0], (((1,), (1,)), ((), ())), preferred_element_type=F32
                )
                half = head % 2 * HD
                folded_ref[head // 2, half:half + HD, :channels] = score_map.astype(BF16)
    for head in range(2 * pairs):
        half = head % 2 * HD
        mixed = maps[2][:, head * HD:(head + 1) * HD].T.astype(BF16)
        blank = jnp.zeros((HD, channels), BF16)
        folded_ref[head // 2, half:half + HD, channels:] = jnp.concatenate(
            [blank, mixed] if head % 2 else [mixed, blank], axis=1
        )


def fold_weights(w_embed, w_qkv):
    channels, width = w_embed.shape
    cols = w_qkv.shape[2]
    wide = 2 * HD
    pairs = cols // wide
    vmem = pl.BlockSpec(memory_space=pltpu.VMEM)
    return pl.pallas_call(
        fold_kernel,
        in_specs=[vmem, vmem],
        out_specs=[vmem, vmem],
        out_shape=[
            jax.ShapeDtypeStruct((pairs, wide, channels + wide), BF16),
            jax.ShapeDtypeStruct((channels, 3 * channels), BF16),
        ],
        scratch_shapes=[
            pltpu.VMEM((2 * channels, width), BF16),
        ],
        compiler_params=pltpu.CompilerParams(vmem_limit_bytes=24 * 1024 * 1024),
        cost_estimate=pl.CostEstimate(
            flops=4 * channels * width * 3 * cols, bytes_accessed=6 * width * cols, transcendentals=0
        ),
        name="fold",
    )(w_embed, w_qkv)


def flow_kernel(counts, place_ref, frozen_ref, read_ref, gram_hbm, embed_hbm, head_hbm, *rest):
    frames, parts = counts
    block_hbm, rest = rest[:frames], rest[frames:]
    folded_hbm, out_hbm, rest = rest[:parts], rest[parts:2 * parts], rest[2 * parts:]
    (result_ref, raw, turned, straight, query, keys, values, mapped, attended,
     folded, w_out, w_head, gram_ref, ready, sems) = rest
    tokens, channels = raw.shape[1:]
    links = read_ref.shape[0]
    slots = links + 1
    pairs_here = folded_hbm[0].shape[0]
    rows_here = out_hbm[0].shape[0]
    hidden = parts * rows_here
    place = place_ref[0]

    block_loads = [
        pltpu.make_async_copy(block_hbm[slot], raw.at[slot], sems.at[slot]) for slot in range(frames)
    ]
    block_loads.append(pltpu.make_async_copy(gram_hbm, gram_ref, sems.at[frames + 2 * parts + 2]))
    folded_loads, late_loads = [], []
    for part in range(parts):
        folded_loads.append(pltpu.make_async_copy(
            folded_hbm[part], folded.at[part * pairs_here:(part + 1) * pairs_here], sems.at[frames + part]))
        late_loads.append(pltpu.make_async_copy(
            out_hbm[part], w_out.at[part * rows_here:(part + 1) * rows_here], sems.at[frames + parts + part]))
    late_loads.append(pltpu.make_async_copy(embed_hbm, w_out.at[hidden:], sems.at[frames + 2 * parts]))
    late_loads.append(pltpu.make_async_copy(head_hbm, w_head, sems.at[frames + 2 * parts + 1]))
    for load in block_loads + folded_loads + late_loads:
        load.start()
    ready[0] = 0

    def await_late():
        @pl.when(ready[0] == 0)
        def _():
            for load in late_loads:
                load.wait()
            ready[0] = 1

    def slot_of(frame):
        return jnp.bitwise_xor(place, frame)

    def ingest(slot, rounded):
        wide = rounded.astype(F32)
        spread = jnp.dot(rounded, gram_ref[...], preferred_element_type=F32)
        spread = spread[:, :channels] + spread[:, channels:2 * channels] + spread[:, 2 * channels:]
        variance = jnp.maximum(jnp.sum(spread * wide, axis=1, keepdims=True), 0.0)
        scaled = (wide * lax.rsqrt(variance + EPSILON)).astype(BF16)
        straight[slot] = scaled
        turned[slot, :channels] = scaled.T
        turned[slot, channels:] = jnp.ones((turned.shape[1] - channels, tokens), BF16)

    for load in block_loads:
        load.wait()
    group = math.gcd(frames, 4)

    def ingest_step(index, carry):
        for side in range(group):
            slot = index * group + side
            ingest(slot, raw[slot])
        return carry

    lax.fori_loop(0, frames // group, ingest_step, 0)
    for load in folded_loads:
        load.wait()

    target = frames - 1 - place
    last = target - 1
    last_safe = jnp.maximum(last, 0)
    run_all = jnp.logical_and(target > 0, frozen_ref[target] == 0)

    def flip():
        rows = lax.broadcasted_iota(jnp.int32, (tokens, tokens), 0)
        cols = lax.broadcasted_iota(jnp.int32, (tokens, tokens), 1)
        return jnp.where(rows + cols == tokens - 1, 1.0, 0.0).astype(BF16)

    def source_of(index):
        return jnp.where(index == 0, last_safe, read_ref[jnp.maximum(index - 1, 0), last_safe])

    def is_run(index):
        frame = source_of(index)
        return jnp.logical_and(frame > 0, frozen_ref[jnp.maximum(frame, 0)] == 0)

    def scores_of(pair, side):
        return jnp.dot(keys[...], mapped[pair, side * HD:(side + 1) * HD], preferred_element_type=F32)

    def context_of(exponents):
        weights = jnp.exp2(exponents).astype(BF16)
        total = jnp.dot(values[...], weights, preferred_element_type=F32)
        mass = total[channels:channels + 1]
        return (total[:channels] / mass).astype(BF16), mass

    def mix(pair, contexts):
        mixed = jnp.dot(
            folded[pair, :, channels:], jnp.concatenate(contexts, axis=0), preferred_element_type=F32
        )
        return mixed.astype(BF16).T

    def attend():
        heads = 2 * folded.shape[0]
        scores, contexts = scores_of(0, 0), []
        fits = jnp.ones((1, tokens), F32)
        for head in range(heads):
            following = scores_of((head + 1) // 2, (head + 1) % 2) if head + 1 < heads else None
            context, mass = context_of(scores)
            fits = jnp.where(jnp.logical_and(mass > 2.0 ** -80, mass < 2.0 ** 110), fits, 0.0)
            contexts.append(context)
            scores = following
            if head % 2:
                pair = head // 2
                attended[:, pair * 2 * HD:(pair + 1) * 2 * HD] = mix(pair, contexts)
                contexts = []

        @pl.when(jnp.min(fits) < 0.5)
        def _():
            def shifted_pair(pair, carry):
                contexts = []
                for side in range(2):
                    scores = scores_of(pair, side)
                    contexts.append(context_of(scores - jnp.max(scores, axis=0, keepdims=True))[0])
                start = pl.multiple_of(pair * 2 * HD, 2 * HD)
                attended[:, pl.ds(start, 2 * HD)] = mix(pair, contexts)
                return carry

            lax.fori_loop(0, folded.shape[0], shifted_pair, 0)

    def evaluate():
        for pair in range(folded.shape[0]):
            mapped[pair] = jnp.dot(
                folded[pair, :, :channels], query[...], preferred_element_type=F32
            ).astype(BF16)
        attend()
        await_late()
        residual = jnp.dot(attended[...], w_out[...], preferred_element_type=F32)
        centred = residual - jnp.mean(residual, axis=1, keepdims=True)
        spread_sq = jnp.mean(centred * centred, axis=1, keepdims=True)
        predicted = jnp.dot(centred.astype(BF16), w_head[...], preferred_element_type=F32)
        return predicted * lax.rsqrt(spread_sq + EPSILON)

    def moved(held, predicted):
        return held * jnp.exp(jnp.tanh(predicted[:, channels:])) + predicted[:, :channels]

    def place_key(index, slot, usable):
        keys[index * tokens:(index + 1) * tokens] = straight[slot]
        block = turned[slot]
        values[:, index * tokens:(index + 1) * tokens] = jnp.where(usable, block, jnp.zeros_like(block))

    def round_step(step, carry):
        final = step == slots

        @pl.when(jnp.logical_and(run_all, jnp.logical_or(final, is_run(jnp.minimum(step, slots - 1)))))
        def _():
            frame = jnp.where(final, last_safe, source_of(jnp.minimum(step, slots - 1)) - 1)
            frame = jnp.maximum(frame, 0)
            own = jnp.where(jnp.logical_and(final, is_run(0)), frames, slot_of(frame))
            attended[:, hidden:] = raw[own]
            query[...] = turned[own, :channels]
            place_key(0, own, True)
            for link in range(links):
                source = read_ref[link, frame]
                usable = source >= 0
                held = slot_of(jnp.maximum(source, 0))
                held = jnp.where(jnp.logical_and(final, is_run(link + 1)), frames + link + 1, held)
                place_key(link + 1, jnp.where(usable, held, own), usable)

            @pl.when(final)
            def _():
                mirror = flip()
                attended[:, hidden:] = jnp.dot(mirror, raw[own], preferred_element_type=F32).astype(BF16)
                query[...] = jnp.dot(query[...], mirror, preferred_element_type=F32).astype(BF16)

            predicted = evaluate()

            @pl.when(jnp.logical_not(final))
            def _():
                base = raw[slot_of(frame + 1)].astype(F32)
                rounded = moved(base, predicted).astype(BF16)
                raw[frames + step] = rounded
                ingest(frames + step, rounded)

            @pl.when(final)
            def _():
                base = jnp.dot(flip(), raw[slot_of(target)], preferred_element_type=F32)
                result_ref[...] = moved(base, predicted)

        return carry

    lax.fori_loop(0, slots + 1, round_step, 0)
    await_late()

    @pl.when(jnp.logical_not(run_all))
    def _():
        result_ref[...] = jnp.dot(flip(), raw[slot_of(target)], preferred_element_type=F32)


def pick_kernel(place_ref, frozen_ref, latent_hbm, context_hbm, picked_ref, rows, sem):
    held = frozen_ref[place_ref[0]] == 1

    @pl.when(held)
    def _():
        pltpu.make_async_copy(context_hbm, rows, sem).start()

    @pl.when(jnp.logical_not(held))
    def _():
        pltpu.make_async_copy(latent_hbm, rows, sem).start()

    pltpu.make_async_copy(latent_hbm, rows, sem).wait()
    picked_ref[...] = rows[...].astype(BF16)


def pick_state(place, frozen, latent, context, cover):
    smem = pl.BlockSpec(memory_space=pltpu.SMEM)
    anywhere = pl.BlockSpec(memory_space=pl.ANY)
    return pl.pallas_call(
        pick_kernel,
        in_specs=[smem, smem, anywhere, anywhere],
        out_specs=pl.BlockSpec(memory_space=pltpu.VMEM),
        out_shape=jax.ShapeDtypeStruct(latent.shape, BF16),
        scratch_shapes=[pltpu.VMEM(latent.shape, F32), pltpu.SemaphoreType.DMA],
        cost_estimate=pl.CostEstimate(flops=cover, bytes_accessed=4 * latent.size, transcendentals=0),
        compiler_params=pltpu.CompilerParams(vmem_limit_bytes=4 * 1024 * 1024),
        name="pick",
    )(place, frozen, latent, context)


def run_flow(place, frozen, read_list, blocks, gram, w_embed, w_head, folded, outs):
    tokens, channels = blocks[0].shape
    frames = len(blocks)
    parts = len(folded)
    slots = read_list.shape[0] + 1
    width = w_embed.shape[1]
    pairs = sum(block.shape[0] for block in folded)
    hidden = sum(block.shape[0] for block in outs)
    vmem = pl.BlockSpec(memory_space=pltpu.VMEM)
    smem = pl.BlockSpec(memory_space=pltpu.SMEM)
    anywhere = pl.BlockSpec(memory_space=pl.ANY)
    held = frames + slots
    hbm = pl.BlockSpec(memory_space=pltpu.HBM)
    return pl.pallas_call(
        functools.partial(flow_kernel, (frames, parts)),
        in_specs=[smem, smem, smem] + [anywhere] * 3 + [hbm] * frames + ([anywhere] + [hbm] * (parts - 1)) * 2,
        out_specs=vmem,
        out_shape=jax.ShapeDtypeStruct((tokens, channels), F32),
        scratch_shapes=[
            pltpu.VMEM((held, tokens, channels), BF16),
            pltpu.VMEM((held, channels + 16, tokens), BF16),
            pltpu.VMEM((held, tokens, channels), BF16),
            pltpu.VMEM((channels, tokens), BF16),
            pltpu.VMEM((slots * tokens, channels), BF16),
            pltpu.VMEM((channels + 16, slots * tokens), BF16),
            pltpu.VMEM((pairs, 2 * HD, tokens), BF16),
            pltpu.VMEM((tokens, hidden + channels), BF16),
            pltpu.VMEM((pairs,) + folded[0].shape[1:], BF16),
            pltpu.VMEM((hidden + channels, width), BF16),
            pltpu.VMEM(w_head.shape, BF16),
            pltpu.VMEM(gram.shape, BF16),
            pltpu.SMEM((1,), jnp.int32),
            pltpu.SemaphoreType.DMA((frames + 3 + 2 * parts,)),
        ],
        compiler_params=pltpu.CompilerParams(vmem_limit_bytes=40 * 1024 * 1024),
        name="flow",
    )(place, frozen, read_list, gram, w_embed, w_head, *blocks, *folded, *outs)


def from_behind(value, axis, shift):
    count = lax.axis_size(axis)
    return lax.ppermute(value, axis, [(source, (source + shift) % count) for source in range(count)])


def across(value, axis, mask):
    return lax.ppermute(value, axis, [(source, source ^ mask) for source in range(lax.axis_size(axis))])


def per_device(latent, context, frozen, read_list, w_embed, w_qkv, w_attn_out, w_head):
    position = lax.axis_index("seq")
    seq_count = lax.axis_size("seq")
    clip_count = lax.axis_size("clip")
    layout = latent.shape
    place = position.reshape(1).astype(jnp.int32)
    rows = (layout[-2], layout[-1])
    held = pick_state(place, frozen, latent.reshape(rows), context.reshape(rows), 6 * w_embed.shape[0] * w_qkv.size)
    blocks = [None] * seq_count
    blocks[0] = held
    for mask in [1] + list(range(2, seq_count, 2)):
        blocks[mask] = across(held, "seq", mask)
    for mask in range(2, seq_count, 2):
        blocks[mask + 1] = across(blocks[mask], "seq", 1)
    outs = [w_attn_out] + [from_behind(w_attn_out, "clip", step) for step in range(1, clip_count)]
    folded, gram = fold_weights(w_embed, w_qkv)
    folded = [folded] + [from_behind(folded, "clip", step) for step in range(1, clip_count)]
    result = run_flow(
        place, frozen, read_list.T, blocks, gram, w_embed, w_head, folded, outs
    )
    return result.reshape(layout)


def solution(mesh):
    return jax.shard_map(
        per_device,
        mesh=mesh,
        in_specs=(
            P(("group", "clip"), "seq", None, None),
            P(("group", "clip"), "seq", None, None),
            P("group"),
            P("group", None),
            P(),
            P(None, None, "clip"),
            P("clip", None),
            P(),
        ),
        out_specs=P(("group", "clip"), "seq", None, None),
        check_vma=False,
    )
```

```python
import functools
import math

import jax
import jax.numpy as jnp
from jax import lax
from jax.experimental import pallas as pl
from jax.experimental.pallas import tpu as pltpu
from jax.sharding import PartitionSpec as P


HD = 128
EPSILON = 1e-05
F32 = jnp.float32
BF16 = jnp.bfloat16


def split_bf16(value, pieces):
    out = []
    for _ in range(pieces):
        piece = value.astype(BF16)
        out.append(piece)
        value = value - piece.astype(F32)
    return out


def fold_kernel(embed_ref, qkv_ref, folded_ref, gram_ref, centred_ref):
    channels, width = embed_ref.shape
    pairs = folded_ref.shape[0]
    rows = embed_ref[...].astype(F32)
    centred = rows - jnp.mean(rows, axis=1, keepdims=True)
    high, low = split_bf16(centred, 2)
    centred_ref[:channels] = high
    centred_ref[channels:] = low
    square = lax.dot_general(
        centred_ref[...], centred_ref[...], (((1,), (1,)), ((), ())), preferred_element_type=F32
    )
    gram = (
        square[:channels, :channels] + square[channels:, channels:]
        + square[:channels, channels:] + square[channels:, :channels]
    ) * (1.0 / width)
    for index, piece in enumerate(split_bf16(gram, 3)):
        gram_ref[:, index * channels:(index + 1) * channels] = piece

    scale = math.log2(math.e) / math.sqrt(HD)
    maps = []
    for index in range(3):
        product = jnp.dot(centred_ref[...], qkv_ref[index], preferred_element_type=F32)
        maps.append(product[:channels] + product[channels:])
        if index == 1:
            for head in range(2 * pairs):
                cols = slice(head * HD, (head + 1) * HD)
                queries = split_bf16(maps[0][:, cols] * scale, 2)
                keys = split_bf16(maps[1][:, cols], 2)
                score_map = lax.dot_general(
                    jnp.concatenate([keys[0], keys[0]], axis=1), jnp.concatenate(queries, axis=1),
                    (((1,), (1,)), ((), ())), preferred_element_type=F32,
                ) + lax.dot_general(
                    keys[1], queries[0], (((1,), (1,)), ((), ())), preferred_element_type=F32
                )
                half = head % 2 * HD
                folded_ref[head // 2, half:half + HD, :channels] = score_map.astype(BF16)
    for head in range(2 * pairs):
        half = head % 2 * HD
        mixed = maps[2][:, head * HD:(head + 1) * HD].T.astype(BF16)
        blank = jnp.zeros((HD, channels), BF16)
        folded_ref[head // 2, half:half + HD, channels:] = jnp.concatenate(
            [blank, mixed] if head % 2 else [mixed, blank], axis=1
        )


def fold_weights(w_embed, w_qkv):
    channels, width = w_embed.shape
    cols = w_qkv.shape[2]
    wide = 2 * HD
    pairs = cols // wide
    vmem = pl.BlockSpec(memory_space=pltpu.VMEM)
    return pl.pallas_call(
        fold_kernel,
        in_specs=[vmem, vmem],
        out_specs=[vmem, vmem],
        out_shape=[
            jax.ShapeDtypeStruct((pairs, wide, channels + wide), BF16),
            jax.ShapeDtypeStruct((channels, 3 * channels), BF16),
        ],
        scratch_shapes=[
            pltpu.VMEM((2 * channels, width), BF16),
        ],
        compiler_params=pltpu.CompilerParams(vmem_limit_bytes=24 * 1024 * 1024),
        cost_estimate=pl.CostEstimate(
            flops=4 * channels * width * 3 * cols, bytes_accessed=6 * width * cols, transcendentals=0
        ),
        name="fold",
    )(w_embed, w_qkv)


def flow_kernel(counts, place_ref, frozen_ref, read_ref, gram_hbm, embed_hbm, head_hbm, *rest):
    frames, parts = counts
    block_hbm, rest = rest[:frames], rest[frames:]
    folded_hbm, out_hbm, rest = rest[:parts], rest[parts:2 * parts], rest[2 * parts:]
    (result_ref, raw, turned, straight, query, keys, values, mapped, attended,
     folded, w_out, w_head, gram_ref, predicted_ref, sems) = rest
    tokens, channels = raw.shape[1:]
    links = read_ref.shape[0]
    slots = links + 1
    pairs_here = folded_hbm[0].shape[0]
    rows_here = out_hbm[0].shape[0]
    hidden = parts * rows_here
    place = place_ref[0]

    block_loads = [
        pltpu.make_async_copy(block_hbm[slot], raw.at[slot], sems.at[slot]) for slot in range(frames)
    ]
    block_loads.append(pltpu.make_async_copy(gram_hbm, gram_ref, sems.at[frames + 2 * parts + 2]))
    folded_loads, late_loads = [], []
    for part in range(parts):
        folded_loads.append(pltpu.make_async_copy(
            folded_hbm[part], folded.at[part * pairs_here:(part + 1) * pairs_here], sems.at[frames + part]))
        late_loads.append(pltpu.make_async_copy(
            out_hbm[part], w_out.at[part * rows_here:(part + 1) * rows_here], sems.at[frames + parts + part]))
    late_loads.append(pltpu.make_async_copy(embed_hbm, w_out.at[hidden:], sems.at[frames + 2 * parts]))
    late_loads.append(pltpu.make_async_copy(head_hbm, w_head, sems.at[frames + 2 * parts + 1]))
    for load in block_loads + folded_loads + late_loads:
        load.start()

    def slot_of(frame):
        return jnp.bitwise_xor(place, frame)

    def ingest(slot, rounded):
        wide = rounded.astype(F32)
        spread = jnp.dot(rounded, gram_ref[...], preferred_element_type=F32)
        spread = spread[:, :channels] + spread[:, channels:2 * channels] + spread[:, 2 * channels:]
        variance = jnp.maximum(jnp.sum(spread * wide, axis=1, keepdims=True), 0.0)
        scaled = (wide * lax.rsqrt(variance + EPSILON)).astype(BF16)
        straight[slot] = scaled
        turned[slot, :channels] = scaled.T
        turned[slot, channels:] = jnp.ones((turned.shape[1] - channels, tokens), BF16)

    for load in block_loads:
        load.wait()
    group = math.gcd(frames, 8)

    def ingest_step(index, carry):
        for side in range(group):
            slot = index * group + side
            ingest(slot, raw[slot])
        return carry

    lax.fori_loop(0, frames // group, ingest_step, 0)
    for load in folded_loads + late_loads:
        load.wait()

    target = frames - 1 - place
    last = target - 1
    last_safe = jnp.maximum(last, 0)
    run_all = jnp.logical_and(target > 0, frozen_ref[target] == 0)

    def flip():
        rows = lax.broadcasted_iota(jnp.int32, (tokens, tokens), 0)
        cols = lax.broadcasted_iota(jnp.int32, (tokens, tokens), 1)
        return jnp.where(rows + cols == tokens - 1, 1.0, 0.0).astype(BF16)

    def source_of(index):
        return jnp.where(index == 0, last_safe, read_ref[jnp.maximum(index - 1, 0), last_safe])

    def is_run(index):
        frame = source_of(index)
        return jnp.logical_and(frame > 0, frozen_ref[jnp.maximum(frame, 0)] == 0)

    def scores_of(pair, side):
        return jnp.dot(keys[...], mapped[pair, side * HD:(side + 1) * HD], preferred_element_type=F32)

    def context_of(exponents):
        weights = jnp.exp2(exponents).astype(BF16)
        total = jnp.dot(values[...], weights, preferred_element_type=F32)
        mass = total[channels:channels + 1]
        return (total[:channels] / mass).astype(BF16), mass

    def mix(pair, contexts):
        mixed = jnp.dot(
            folded[pair, :, channels:], jnp.concatenate(contexts, axis=0), preferred_element_type=F32
        )
        return mixed.astype(BF16).T

    def attend():
        heads = 2 * folded.shape[0]
        queue, contexts = [scores_of(0, 0), scores_of(0, 1)], []
        fits = jnp.ones((1, tokens), F32)
        for head in range(heads):
            if head + 2 < heads:
                queue.append(scores_of((head + 2) // 2, head % 2))
            context, mass = context_of(queue.pop(0))
            fits = jnp.where(jnp.logical_and(mass > 2.0 ** -80, mass < 2.0 ** 110), fits, 0.0)
            contexts.append(context)
            if head % 2:
                pair = head // 2
                attended[:, pair * 2 * HD:(pair + 1) * 2 * HD] = mix(pair, contexts)
                contexts = []

        return jnp.min(fits)

    def attend_shifted():
        def shifted_pair(pair, carry):
            contexts = []
            for side in range(2):
                scores = scores_of(pair, side)
                contexts.append(context_of(scores - jnp.max(scores, axis=0, keepdims=True))[0])
            start = pl.multiple_of(pair * 2 * HD, 2 * HD)
            attended[:, pl.ds(start, 2 * HD)] = mix(pair, contexts)
            return carry

        lax.fori_loop(0, folded.shape[0], shifted_pair, 0)

    def evaluate():
        for pair in range(folded.shape[0]):
            mapped[pair] = jnp.dot(
                folded[pair, :, :channels], query[...], preferred_element_type=F32
            ).astype(BF16)
        fits = attend()
        predicted_ref[...] = predict()

        @pl.when(fits < 0.5)
        def _():
            attend_shifted()
            predicted_ref[...] = predict()

        return predicted_ref[...]

    def predict():
        halves = [slice(start, start + tokens // 2) for start in (0, tokens // 2)]
        residuals = [jnp.dot(attended[rows], w_out[...], preferred_element_type=F32) for rows in halves]
        return jnp.concatenate([finish(residual) for residual in residuals], axis=0)

    def finish(residual):
        centred = residual - jnp.mean(residual, axis=1, keepdims=True)
        spread_sq = jnp.mean(centred * centred, axis=1, keepdims=True)
        predicted = jnp.dot(centred.astype(BF16), w_head[...], preferred_element_type=F32)
        return predicted * lax.rsqrt(spread_sq + EPSILON)

    def moved(held, predicted):
        return held * jnp.exp(jnp.tanh(predicted[:, channels:])) + predicted[:, :channels]

    def place_key(index, slot, usable):
        keys[index * tokens:(index + 1) * tokens] = straight[slot]
        block = turned[slot]
        values[:, index * tokens:(index + 1) * tokens] = jnp.where(usable, block, jnp.zeros_like(block))

    def round_step(step, carry):
        final = step == slots

        @pl.when(jnp.logical_and(run_all, jnp.logical_or(final, is_run(jnp.minimum(step, slots - 1)))))
        def _():
            frame = jnp.where(final, last_safe, source_of(jnp.minimum(step, slots - 1)) - 1)
            frame = jnp.maximum(frame, 0)
            own = jnp.where(jnp.logical_and(final, is_run(0)), frames, slot_of(frame))
            attended[:, hidden:] = raw[own]
            query[...] = turned[own, :channels]
            place_key(0, own, True)
            for link in range(links):
                source = read_ref[link, frame]
                usable = source >= 0
                held = slot_of(jnp.maximum(source, 0))
                held = jnp.where(jnp.logical_and(final, is_run(link + 1)), frames + link + 1, held)
                place_key(link + 1, jnp.where(usable, held, own), usable)

            @pl.when(final)
            def _():
                mirror = flip()
                attended[:, hidden:] = jnp.dot(mirror, raw[own], preferred_element_type=F32).astype(BF16)
                query[...] = jnp.dot(query[...], mirror, preferred_element_type=F32).astype(BF16)

            predicted = evaluate()

            @pl.when(jnp.logical_not(final))
            def _():
                base = raw[slot_of(frame + 1)].astype(F32)
                rounded = moved(base, predicted).astype(BF16)
                raw[frames + step] = rounded
                ingest(frames + step, rounded)

            @pl.when(final)
            def _():
                base = jnp.dot(flip(), raw[slot_of(target)], preferred_element_type=F32)
                result_ref[...] = moved(base, predicted)

        return carry

    lax.fori_loop(0, slots + 1, round_step, 0)

    @pl.when(jnp.logical_not(run_all))
    def _():
        result_ref[...] = jnp.dot(flip(), raw[slot_of(target)], preferred_element_type=F32)


def pick_kernel(place_ref, frozen_ref, latent_hbm, context_hbm, picked_ref, rows, sem):
    held = frozen_ref[place_ref[0]] == 1

    @pl.when(held)
    def _():
        pltpu.make_async_copy(context_hbm, rows, sem).start()

    @pl.when(jnp.logical_not(held))
    def _():
        pltpu.make_async_copy(latent_hbm, rows, sem).start()

    pltpu.make_async_copy(latent_hbm, rows, sem).wait()
    picked_ref[...] = rows[...].astype(BF16)


def pick_state(place, frozen, latent, context, cover):
    smem = pl.BlockSpec(memory_space=pltpu.SMEM)
    anywhere = pl.BlockSpec(memory_space=pl.ANY)
    return pl.pallas_call(
        pick_kernel,
        in_specs=[smem, smem, anywhere, anywhere],
        out_specs=pl.BlockSpec(memory_space=pltpu.VMEM),
        out_shape=jax.ShapeDtypeStruct(latent.shape, BF16),
        scratch_shapes=[pltpu.VMEM(latent.shape, F32), pltpu.SemaphoreType.DMA],
        cost_estimate=pl.CostEstimate(flops=cover, bytes_accessed=4 * latent.size, transcendentals=0),
        compiler_params=pltpu.CompilerParams(vmem_limit_bytes=4 * 1024 * 1024),
        name="pick",
    )(place, frozen, latent, context)


def run_flow(place, frozen, read_list, blocks, gram, w_embed, w_head, folded, outs):
    tokens, channels = blocks[0].shape
    frames = len(blocks)
    parts = len(folded)
    slots = read_list.shape[0] + 1
    width = w_embed.shape[1]
    pairs = sum(block.shape[0] for block in folded)
    hidden = sum(block.shape[0] for block in outs)
    vmem = pl.BlockSpec(memory_space=pltpu.VMEM)
    smem = pl.BlockSpec(memory_space=pltpu.SMEM)
    anywhere = pl.BlockSpec(memory_space=pl.ANY)
    held = frames + slots
    hbm = pl.BlockSpec(memory_space=pltpu.HBM)
    return pl.pallas_call(
        functools.partial(flow_kernel, (frames, parts)),
        in_specs=[smem, smem, smem] + [anywhere] * 3 + [hbm] * frames + ([anywhere] + [hbm] * (parts - 1)) * 2,
        out_specs=vmem,
        out_shape=jax.ShapeDtypeStruct((tokens, channels), F32),
        scratch_shapes=[
            pltpu.VMEM((held, tokens, channels), BF16),
            pltpu.VMEM((held, channels + 16, tokens), BF16),
            pltpu.VMEM((held, tokens, channels), BF16),
            pltpu.VMEM((channels, tokens), BF16),
            pltpu.VMEM((slots * tokens, channels), BF16),
            pltpu.VMEM((channels + 16, slots * tokens), BF16),
            pltpu.VMEM((pairs, 2 * HD, tokens), BF16),
            pltpu.VMEM((tokens, hidden + channels), BF16),
            pltpu.VMEM((pairs,) + folded[0].shape[1:], BF16),
            pltpu.VMEM((hidden + channels, width), BF16),
            pltpu.VMEM(w_head.shape, BF16),
            pltpu.VMEM(gram.shape, BF16),
            pltpu.VMEM((tokens, w_head.shape[1]), F32),
            pltpu.SemaphoreType.DMA((frames + 3 + 2 * parts,)),
        ],
        compiler_params=pltpu.CompilerParams(vmem_limit_bytes=40 * 1024 * 1024),
        name="flow",
    )(place, frozen, read_list, gram, w_embed, w_head, *blocks, *folded, *outs)


def from_behind(value, axis, shift):
    count = lax.axis_size(axis)
    return lax.ppermute(value, axis, [(source, (source + shift) % count) for source in range(count)])


def across(value, axis, mask):
    return lax.ppermute(value, axis, [(source, source ^ mask) for source in range(lax.axis_size(axis))])


def per_device(latent, context, frozen, read_list, w_embed, w_qkv, w_attn_out, w_head):
    position = lax.axis_index("seq")
    seq_count = lax.axis_size("seq")
    clip_count = lax.axis_size("clip")
    layout = latent.shape
    place = position.reshape(1).astype(jnp.int32)
    rows = (layout[-2], layout[-1])
    held = pick_state(place, frozen, latent.reshape(rows), context.reshape(rows), 6 * w_embed.shape[0] * w_qkv.size)
    blocks = [None] * seq_count
    blocks[0] = held
    for mask in [1] + list(range(2, seq_count, 2)):
        blocks[mask] = across(held, "seq", mask)
    for mask in range(2, seq_count, 2):
        blocks[mask + 1] = across(blocks[mask], "seq", 1)
    outs = [w_attn_out] + [from_behind(w_attn_out, "clip", step) for step in range(1, clip_count)]
    folded, gram = fold_weights(w_embed, w_qkv)
    folded = [folded] + [from_behind(folded, "clip", step) for step in range(1, clip_count)]
    result = run_flow(
        place, frozen, read_list.T, blocks, gram, w_embed, w_head, folded, outs
    )
    return result.reshape(layout)


def solution(mesh):
    return jax.shard_map(
        per_device,
        mesh=mesh,
        in_specs=(
            P(("group", "clip"), "seq", None, None),
            P(("group", "clip"), "seq", None, None),
            P("group"),
            P("group", None),
            P(),
            P(None, None, "clip"),
            P("clip", None),
            P(),
        ),
        out_specs=P(("group", "clip"), "seq", None, None),
        check_vma=False,
    )
```

```python
import functools
import math

import jax
import jax.numpy as jnp
from jax import lax
from jax.experimental import pallas as pl
from jax.experimental.pallas import tpu as pltpu
from jax.sharding import PartitionSpec as P


HD = 128
EPSILON = 1e-05
F32 = jnp.float32
BF16 = jnp.bfloat16


def split_bf16(value, pieces):
    out = []
    for _ in range(pieces):
        piece = value.astype(BF16)
        out.append(piece)
        value = value - piece.astype(F32)
    return out


def fold_kernel(embed_ref, qkv_ref, folded_ref, gram_ref, centred_ref):
    channels, width = embed_ref.shape
    pairs = folded_ref.shape[0]
    rows = embed_ref[...].astype(F32)
    centred = rows - jnp.mean(rows, axis=1, keepdims=True)
    high, low = split_bf16(centred, 2)
    centred_ref[:channels] = high
    centred_ref[channels:] = low
    square = lax.dot_general(
        centred_ref[...], centred_ref[...], (((1,), (1,)), ((), ())), preferred_element_type=F32
    )
    gram = (
        square[:channels, :channels] + square[channels:, channels:]
        + square[:channels, channels:] + square[channels:, :channels]
    ) * (1.0 / width)
    for index, piece in enumerate(split_bf16(gram, 3)):
        gram_ref[:, index * channels:(index + 1) * channels] = piece

    scale = math.log2(math.e) / math.sqrt(HD)
    maps = []
    for index in range(3):
        product = jnp.dot(centred_ref[...], qkv_ref[index], preferred_element_type=F32)
        maps.append(product[:channels] + product[channels:])
        if index == 1:
            for head in range(2 * pairs):
                cols = slice(head * HD, (head + 1) * HD)
                queries = split_bf16(maps[0][:, cols] * scale, 2)
                keys = split_bf16(maps[1][:, cols], 2)
                score_map = lax.dot_general(
                    jnp.concatenate([keys[0], keys[0]], axis=1), jnp.concatenate(queries, axis=1),
                    (((1,), (1,)), ((), ())), preferred_element_type=F32,
                ) + lax.dot_general(
                    keys[1], queries[0], (((1,), (1,)), ((), ())), preferred_element_type=F32
                )
                half = head % 2 * HD
                folded_ref[head // 2, half:half + HD, :channels] = score_map.astype(BF16)
    for head in range(2 * pairs):
        half = head % 2 * HD
        mixed = maps[2][:, head * HD:(head + 1) * HD].T.astype(BF16)
        blank = jnp.zeros((HD, channels), BF16)
        folded_ref[head // 2, half:half + HD, channels:] = jnp.concatenate(
            [blank, mixed] if head % 2 else [mixed, blank], axis=1
        )


def fold_weights(w_embed, w_qkv):
    channels, width = w_embed.shape
    cols = w_qkv.shape[2]
    wide = 2 * HD
    pairs = cols // wide
    vmem = pl.BlockSpec(memory_space=pltpu.VMEM)
    return pl.pallas_call(
        fold_kernel,
        in_specs=[vmem, vmem],
        out_specs=[vmem, vmem],
        out_shape=[
            jax.ShapeDtypeStruct((pairs, wide, channels + wide), BF16),
            jax.ShapeDtypeStruct((channels, 3 * channels), BF16),
        ],
        scratch_shapes=[
            pltpu.VMEM((2 * channels, width), BF16),
        ],
        compiler_params=pltpu.CompilerParams(vmem_limit_bytes=24 * 1024 * 1024),
        cost_estimate=pl.CostEstimate(
            flops=4 * channels * width * 3 * cols, bytes_accessed=6 * width * cols, transcendentals=0
        ),
        name="fold",
    )(w_embed, w_qkv)


def flow_kernel(counts, place_ref, frozen_ref, read_ref, gram_hbm, embed_hbm, head_hbm, *rest):
    frames, parts = counts
    block_hbm, rest = rest[:frames], rest[frames:]
    folded_hbm, out_hbm, rest = rest[:parts], rest[parts:2 * parts], rest[2 * parts:]
    (result_ref, raw, turned, straight, query, keys, values, mapped, attended,
     folded, w_out, w_head, gram_ref, predicted_ref, sems) = rest
    tokens, channels = raw.shape[1:]
    links = read_ref.shape[0]
    slots = links + 1
    pairs_here = folded_hbm[0].shape[0]
    rows_here = out_hbm[0].shape[0]
    hidden = parts * rows_here
    place = place_ref[0]

    block_loads = [
        pltpu.make_async_copy(block_hbm[slot], raw.at[slot], sems.at[slot]) for slot in range(frames)
    ]
    block_loads.append(pltpu.make_async_copy(gram_hbm, gram_ref, sems.at[frames + 2 * parts + 2]))
    folded_loads, late_loads = [], []
    for part in range(parts):
        folded_loads.append(pltpu.make_async_copy(
            folded_hbm[part], folded.at[part * pairs_here:(part + 1) * pairs_here], sems.at[frames + part]))
        late_loads.append(pltpu.make_async_copy(
            out_hbm[part], w_out.at[part * rows_here:(part + 1) * rows_here], sems.at[frames + parts + part]))
    late_loads.append(pltpu.make_async_copy(embed_hbm, w_out.at[hidden:], sems.at[frames + 2 * parts]))
    late_loads.append(pltpu.make_async_copy(head_hbm, w_head, sems.at[frames + 2 * parts + 1]))
    for load in block_loads + folded_loads + late_loads:
        load.start()

    def slot_of(frame):
        return jnp.bitwise_xor(place, frame)

    def ingest(slot, rounded):
        wide = rounded.astype(F32)
        spread = jnp.dot(rounded, gram_ref[...], preferred_element_type=F32)
        spread = spread[:, :channels] + spread[:, channels:2 * channels] + spread[:, 2 * channels:]
        variance = jnp.maximum(jnp.sum(spread * wide, axis=1, keepdims=True), 0.0)
        scaled = (wide * lax.rsqrt(variance + EPSILON)).astype(BF16)
        straight[slot] = scaled
        turned[slot, :channels] = scaled.T
        turned[slot, channels:] = jnp.ones((turned.shape[1] - channels, tokens), BF16)

    for load in block_loads:
        load.wait()
    group = math.gcd(frames, 8)

    def ingest_step(index, carry):
        for side in range(group):
            slot = index * group + side
            ingest(slot, raw[slot])
        return carry

    lax.fori_loop(0, frames // group, ingest_step, 0)
    for load in folded_loads + late_loads:
        load.wait()

    target = frames - 1 - place
    last = target - 1
    last_safe = jnp.maximum(last, 0)
    run_all = jnp.logical_and(target > 0, frozen_ref[target] == 0)

    def flip():
        rows = lax.broadcasted_iota(jnp.int32, (tokens, tokens), 0)
        cols = lax.broadcasted_iota(jnp.int32, (tokens, tokens), 1)
        return jnp.where(rows + cols == tokens - 1, 1.0, 0.0).astype(BF16)

    def source_of(index):
        return jnp.where(index == 0, last_safe, read_ref[jnp.maximum(index - 1, 0), last_safe])

    def is_run(index):
        frame = source_of(index)
        return jnp.logical_and(frame > 0, frozen_ref[jnp.maximum(frame, 0)] == 0)

    def scores_of(pair, side):
        return jnp.dot(keys[...], mapped[pair, side * HD:(side + 1) * HD], preferred_element_type=F32)

    def context_of(exponents):
        weights = jnp.exp2(exponents).astype(BF16)
        total = jnp.dot(values[...], weights, preferred_element_type=F32)
        mass = total[channels:channels + 1]
        return (total[:channels] / mass).astype(BF16), mass

    def mix(pair, contexts):
        mixed = jnp.dot(
            folded[pair, :, channels:], jnp.concatenate(contexts, axis=0), preferred_element_type=F32
        )
        return mixed.astype(BF16).T

    def attend():
        heads = 2 * folded.shape[0]
        queue, contexts = [scores_of(0, 0), scores_of(0, 1)], []
        fits = jnp.ones((1, tokens), F32)
        for head in range(heads):
            if head + 2 < heads:
                queue.append(scores_of((head + 2) // 2, head % 2))
            context, mass = context_of(queue.pop(0))
            fits = jnp.where(jnp.logical_and(mass > 2.0 ** -80, mass < 2.0 ** 110), fits, 0.0)
            contexts.append(context)
            if head % 2:
                pair = head // 2
                attended[:, pair * 2 * HD:(pair + 1) * 2 * HD] = mix(pair, contexts)
                contexts = []

        return jnp.min(fits)

    def attend_shifted():
        def shifted_pair(pair, carry):
            contexts = []
            for side in range(2):
                scores = scores_of(pair, side)
                contexts.append(context_of(scores - jnp.max(scores, axis=0, keepdims=True))[0])
            start = pl.multiple_of(pair * 2 * HD, 2 * HD)
            attended[:, pl.ds(start, 2 * HD)] = mix(pair, contexts)
            return carry

        lax.fori_loop(0, folded.shape[0], shifted_pair, 0)

    def evaluate():
        for pair in range(folded.shape[0]):
            mapped[pair] = jnp.dot(
                folded[pair, :, :channels], query[...], preferred_element_type=F32
            ).astype(BF16)
        fits = attend()
        predicted_ref[...] = predict()

        @pl.when(fits < 0.5)
        def _():
            attend_shifted()
            predicted_ref[...] = predict()

        return predicted_ref[...]

    def predict():
        halves = [slice(start, start + tokens // 2) for start in (0, tokens // 2)]
        residuals = [jnp.dot(attended[rows], w_out[...], preferred_element_type=F32) for rows in halves]
        return jnp.concatenate([finish(residual) for residual in residuals], axis=0)

    def finish(residual):
        centred = residual - jnp.mean(residual, axis=1, keepdims=True)
        spread_sq = jnp.mean(centred * centred, axis=1, keepdims=True)
        predicted = jnp.dot(centred.astype(BF16), w_head[...], preferred_element_type=F32)
        return predicted * lax.rsqrt(spread_sq + EPSILON)

    def moved(held, predicted):
        return held * jnp.exp(jnp.tanh(predicted[:, channels:])) + predicted[:, :channels]

    def place_key(index, slot, usable):
        keys[index * tokens:(index + 1) * tokens] = straight[slot]
        block = turned[slot]
        values[:, index * tokens:(index + 1) * tokens] = jnp.where(usable, block, jnp.zeros_like(block))

    def round_step(step, carry):
        final = step == slots

        @pl.when(jnp.logical_and(run_all, jnp.logical_or(final, is_run(jnp.minimum(step, slots - 1)))))
        def _():
            frame = jnp.where(final, last_safe, source_of(jnp.minimum(step, slots - 1)) - 1)
            frame = jnp.maximum(frame, 0)
            own = jnp.where(jnp.logical_and(final, is_run(0)), frames, slot_of(frame))
            attended[:, hidden:] = raw[own]
            query[...] = turned[own, :channels]
            place_key(0, own, True)
            for link in range(links):
                source = read_ref[link, frame]
                usable = source >= 0
                held = slot_of(jnp.maximum(source, 0))
                held = jnp.where(jnp.logical_and(final, is_run(link + 1)), frames + link + 1, held)
                place_key(link + 1, jnp.where(usable, held, own), usable)

            @pl.when(final)
            def _():
                mirror = flip()
                attended[:, hidden:] = jnp.dot(mirror, raw[own], preferred_element_type=F32).astype(BF16)
                query[...] = jnp.dot(query[...], mirror, preferred_element_type=F32).astype(BF16)

            predicted = evaluate()

            @pl.when(jnp.logical_not(final))
            def _():
                base = raw[slot_of(frame + 1)].astype(F32)
                rounded = moved(base, predicted).astype(BF16)
                raw[frames + step] = rounded
                ingest(frames + step, rounded)

            @pl.when(final)
            def _():
                base = jnp.dot(flip(), raw[slot_of(target)], preferred_element_type=F32)
                result_ref[...] = moved(base, predicted)

        return carry

    lax.fori_loop(0, slots + 1, round_step, 0)

    @pl.when(jnp.logical_not(run_all))
    def _():
        result_ref[...] = jnp.dot(flip(), raw[slot_of(target)], preferred_element_type=F32)


def pick_kernel(place_ref, frozen_hbm, latent_hbm, context_hbm, picked_ref, rows, flags, sem, flag_sem):
    flag_load = pltpu.make_async_copy(frozen_hbm, flags, flag_sem)
    row_loads = [
        pltpu.make_async_copy(latent_hbm, rows.at[0], sem.at[0]),
        pltpu.make_async_copy(context_hbm, rows.at[1], sem.at[1]),
    ]
    for load in [flag_load] + row_loads:
        load.start()
    for load in [flag_load] + row_loads:
        load.wait()
    picked_ref[...] = rows[jnp.where(flags[place_ref[0]] == 1, 1, 0)].astype(BF16)


def pick_state(place, frozen, latent, context, cover):
    smem = pl.BlockSpec(memory_space=pltpu.SMEM)
    hbm = pl.BlockSpec(memory_space=pltpu.HBM)
    return pl.pallas_call(
        pick_kernel,
        in_specs=[smem, hbm, hbm, hbm],
        out_specs=pl.BlockSpec(memory_space=pltpu.VMEM),
        out_shape=jax.ShapeDtypeStruct(latent.shape, BF16),
        scratch_shapes=[
            pltpu.VMEM((2,) + latent.shape, F32),
            pltpu.SMEM(frozen.shape, jnp.int32),
            pltpu.SemaphoreType.DMA((2,)),
            pltpu.SemaphoreType.DMA,
        ],
        cost_estimate=pl.CostEstimate(flops=cover, bytes_accessed=4 * latent.size, transcendentals=0),
        compiler_params=pltpu.CompilerParams(vmem_limit_bytes=4 * 1024 * 1024),
        name="pick",
    )(
        place,
        pltpu.with_memory_space_constraint(frozen, pltpu.HBM),
        pltpu.with_memory_space_constraint(latent, pltpu.HBM),
        pltpu.with_memory_space_constraint(context, pltpu.HBM),
    )


def run_flow(place, frozen, read_list, blocks, gram, w_embed, w_head, folded, outs):
    tokens, channels = blocks[0].shape
    frames = len(blocks)
    parts = len(folded)
    slots = read_list.shape[0] + 1
    width = w_embed.shape[1]
    pairs = sum(block.shape[0] for block in folded)
    hidden = sum(block.shape[0] for block in outs)
    vmem = pl.BlockSpec(memory_space=pltpu.VMEM)
    smem = pl.BlockSpec(memory_space=pltpu.SMEM)
    anywhere = pl.BlockSpec(memory_space=pl.ANY)
    held = frames + slots
    hbm = pl.BlockSpec(memory_space=pltpu.HBM)
    return pl.pallas_call(
        functools.partial(flow_kernel, (frames, parts)),
        in_specs=[smem, smem, smem] + [anywhere] * 3 + [hbm] * frames + ([anywhere] + [hbm] * (parts - 1)) * 2,
        out_specs=vmem,
        out_shape=jax.ShapeDtypeStruct((tokens, channels), F32),
        scratch_shapes=[
            pltpu.VMEM((held, tokens, channels), BF16),
            pltpu.VMEM((held, channels + 16, tokens), BF16),
            pltpu.VMEM((held, tokens, channels), BF16),
            pltpu.VMEM((channels, tokens), BF16),
            pltpu.VMEM((slots * tokens, channels), BF16),
            pltpu.VMEM((channels + 16, slots * tokens), BF16),
            pltpu.VMEM((pairs, 2 * HD, tokens), BF16),
            pltpu.VMEM((tokens, hidden + channels), BF16),
            pltpu.VMEM((pairs,) + folded[0].shape[1:], BF16),
            pltpu.VMEM((hidden + channels, width), BF16),
            pltpu.VMEM(w_head.shape, BF16),
            pltpu.VMEM(gram.shape, BF16),
            pltpu.VMEM((tokens, w_head.shape[1]), F32),
            pltpu.SemaphoreType.DMA((frames + 3 + 2 * parts,)),
        ],
        compiler_params=pltpu.CompilerParams(vmem_limit_bytes=40 * 1024 * 1024),
        name="flow",
    )(place, frozen, read_list, gram, w_embed, w_head, *blocks, *folded, *outs)


def from_behind(value, axis, shift):
    count = lax.axis_size(axis)
    return lax.ppermute(value, axis, [(source, (source + shift) % count) for source in range(count)])


def across(value, axis, mask):
    return lax.ppermute(value, axis, [(source, source ^ mask) for source in range(lax.axis_size(axis))])


def per_device(latent, context, frozen, read_list, w_embed, w_qkv, w_attn_out, w_head):
    position = lax.axis_index("seq")
    seq_count = lax.axis_size("seq")
    clip_count = lax.axis_size("clip")
    layout = latent.shape
    place = position.reshape(1).astype(jnp.int32)
    rows = (layout[-2], layout[-1])
    held = pick_state(place, frozen, latent.reshape(rows), context.reshape(rows), 6 * w_embed.shape[0] * w_qkv.size)
    blocks = [None] * seq_count
    blocks[0] = held
    for mask in [1] + list(range(2, seq_count, 2)):
        blocks[mask] = across(held, "seq", mask)
    for mask in range(2, seq_count, 2):
        blocks[mask + 1] = across(blocks[mask], "seq", 1)
    outs = [w_attn_out] + [from_behind(w_attn_out, "clip", step) for step in range(1, clip_count)]
    folded, gram = fold_weights(w_embed, w_qkv)
    folded = [folded] + [from_behind(folded, "clip", step) for step in range(1, clip_count)]
    result = run_flow(
        place, frozen, read_list.T, blocks, gram, w_embed, w_head, folded, outs
    )
    return result.reshape(layout)


def solution(mesh):
    return jax.shard_map(
        per_device,
        mesh=mesh,
        in_specs=(
            P(("group", "clip"), "seq", None, None),
            P(("group", "clip"), "seq", None, None),
            P("group"),
            P("group", None),
            P(),
            P(None, None, "clip"),
            P("clip", None),
            P(),
        ),
        out_specs=P(("group", "clip"), "seq", None, None),
        check_vma=False,
    )
```
